32 devices in a mesh: rows: 8 (over y, x, core), cols: 4 (over z).
Axes of the slice: x: 2, y: 2, z: 4, core: 2. Of those that a mesh axis runs over, the one named last changes fastest.
Arguments:
- latent: float32 [1, 512, 512, 128], P(None, 'rows', 'cols'), may hold values from -6 to 6
- w_small: float32 [512, 128], replicated, may hold values from -0.25 to 0.25
- w_large: float32 [2048, 128], replicated, may hold values from -0.125 to 0.125
- gain_embed: float32 [256], replicated, may hold values from 0.1 to 1.9
- gain_attn: float32 [256], replicated, may hold values from 0.1 to 1.9
- w_qkv: float32 [256, 768], replicated, may hold values from -8 to 8
- pos_bias: float32 [8, 16, 16], replicated, may hold values from -4 to 4
- w_proj: float32 [256, 256], replicated, may hold values from -0.375 to 0.375
- gain_mlp: float32 [256], replicated, may hold values from 0.1 to 1.9
- w_up: float32 [256, 1024], replicated, may hold values from -0.375 to 0.375
- w_down: float32 [1024, 256], replicated, may hold values from -0.1875 to 0.1875
Outputs:
- result: float32 [1, 256, 256, 256], P(None, 'rows', 'cols')
The draws below stay inside these ranges and needn't reach their ends.
All inputs are finite; a program needn't handle non-finite values.
Results may differ from the reference program's by a relative error of at most 0.0003.
Values sent between devices are 32-bit elements; how exact they have to be, the bound alone decides.
A program may use at most 192 MiB of HBM per device.

```python
import jax
import jax.numpy as jnp
from jax import lax

BATCH = 1
INTV = 64
CIN = 128
C = 256
HEADS = 8
FF = 1024
CE = 128
HD = 32
H = 256
W = 256
GR = 4
GT = 16


def draw_w_qkv(key, part):
    base = jax.random.normal(key, (C, 3 * C), jnp.float32) / jnp.sqrt(jnp.float32(C))
    return jnp.clip(base, -8.0, 8.0)


def block_scale(rng, shape, pieces, smallest, high):
    level = 1.0
    for position, shards_of in pieces:
        draws = jax.random.uniform(jax.random.fold_in(jax.random.fold_in(rng, 6), position), (shards_of,), jnp.float32, smallest / len(pieces), high / len(pieces))
        level = level * jnp.repeat(jnp.exp(draws), shape[position] // shards_of).reshape((-1,) + (1,) * (len(shape) - 1 - position))
    return level


def scatter_about(own_key, extent, scale, reach, split=(), kind=jnp.bfloat16):
    entries = scale * jax.random.normal(own_key, extent, jnp.float32)
    if split:
        entries = entries * block_scale(own_key, extent, split, -0.22, 0.18)
    return jnp.clip(entries, -reach, reach).astype(kind)


def setup_inputs(seed: int = 0) -> dict:
    streams_of = jax.random.split(jax.random.key(seed), 12)
    return {
        "latent": scatter_about(streams_of[0], (BATCH, 2 * H, 2 * W, CIN), 1.0, 6.0, ((1, 8), (2, 4)), jnp.float32),
        "w_small": scatter_about(streams_of[1], (4 * CIN, CE), (4 * CIN) ** -0.5, 0.25, (), jnp.float32),
        "w_large": scatter_about(streams_of[2], (16 * CIN, CE), (16 * CIN) ** -0.5, 0.125, (), jnp.float32),
        "gain_embed": jnp.clip(1.0 + 0.18 * jax.random.normal(streams_of[3], (C,), jnp.float32), 0.1, 1.9),
        "gain_attn": jnp.clip(1.0 + 0.18 * jax.random.normal(streams_of[4], (C,), jnp.float32), 0.1, 1.9),
        "w_qkv": draw_w_qkv(jax.random.fold_in(streams_of[11], 71), 0),
        "pos_bias": scatter_about(streams_of[6], (HEADS, GT, GT), 1.0, 4.0, (), jnp.float32),
        "w_proj": scatter_about(streams_of[7], (C, C), C ** -0.5, 0.375, (), jnp.float32),
        "gain_mlp": jnp.clip(1.0 + 0.18 * jax.random.normal(streams_of[8], (C,), jnp.float32), 0.1, 1.9),
        "w_up": scatter_about(streams_of[9], (C, FF), C ** -0.5, 0.375, (), jnp.float32),
        "w_down": scatter_about(streams_of[10], (FF, C), FF ** -0.5, 0.1875, (), jnp.float32),
    }


def matmul(left, right):
    return jnp.dot(left, right, precision=lax.Precision.HIGHEST, preferred_element_type=jnp.float32)

def layer_norm(values, gain):
    center = values - lax.optimization_barrier(jnp.mean(values, axis=-1, keepdims=True))
    spread = lax.optimization_barrier(jnp.mean(center * center, axis=-1, keepdims=True))
    return center * lax.rsqrt(spread + 1e-05) * gain

def reference(latent, w_small, w_large, gain_embed, gain_attn, w_qkv, pos_bias, w_proj, gain_mlp, w_up, w_down):
    patches = latent.reshape(BATCH, H, 2, W, 2, CIN).transpose(0, 1, 3, 2, 4, 5).reshape(-1, 4 * CIN)
    small = matmul(patches, w_small)
    padded = jnp.pad(latent, ((0, 0), (1, 1), (1, 1), (0, 0)))
    large = jnp.zeros((BATCH * H * W, CE), jnp.float32)
    for row_shift in range(4):
        for col_shift in range(4):
            piece = padded[:, row_shift:row_shift + 2 * H:2, col_shift:col_shift + 2 * W:2, :].reshape(-1, CIN)
            first = (row_shift * 4 + col_shift) * CIN
            large = large + matmul(piece, w_large[first:first + CIN])
    embedded = layer_norm(jnp.concatenate([small, large], axis=-1), gain_embed)
    grouped = embedded.reshape(BATCH, GR, INTV, W // INTV, INTV, C).transpose(0, 2, 4, 1, 3, 5)
    grouped = grouped.reshape(BATCH * INTV, INTV, GT, C)
    scale = 1.0 / jnp.sqrt(jnp.float32(HD))

    def block(tokens):
        normed = layer_norm(tokens, gain_attn)
        qkv = matmul(normed.reshape(-1, C), w_qkv).reshape(INTV, GT, 3, HEADS, HD)
        scores = jnp.einsum('gqhd,gkhd->ghqk', qkv[:, :, 0], qkv[:, :, 1], precision=lax.Precision.HIGHEST) * scale + pos_bias[None]
        top = lax.optimization_barrier(jnp.max(scores, axis=-1, keepdims=True))
        expd = jnp.exp(scores - top)
        probs = expd / lax.optimization_barrier(jnp.sum(expd, axis=-1, keepdims=True))
        mixed = jnp.einsum('ghqk,gkhd->gqhd', probs, qkv[:, :, 2], precision=lax.Precision.HIGHEST).reshape(-1, C)
        after = tokens.reshape(-1, C) + matmul(mixed, w_proj)
        hidden = jax.nn.gelu(matmul(layer_norm(after, gain_mlp), w_up), approximate=False)
        return (after + matmul(hidden, w_down)).reshape(INTV, GT, C)
    output = lax.map(block, grouped)
    output = output.reshape(BATCH, INTV, INTV, GR, W // INTV, C).transpose(0, 3, 1, 4, 2, 5)
    return output.reshape(BATCH, H, W, C)
```

```python
import functools

import jax
import jax.numpy as jnp
from jax import lax
from jax.experimental import pallas as pl
from jax.experimental.pallas import tpu as pltpu
from jax.sharding import PartitionSpec as P

HEADS = 8
STAGES = 4
MESH = pl.DeviceIdType.MESH
F32 = jnp.float32
BF16 = jnp.bfloat16


def split(values):
    high = values.astype(BF16)
    return high, (values - high.astype(F32)).astype(BF16)


def dot(left, right, dims=((1,), (0,))):
    return lax.dot_general(left, right, (dims, ((), ())), preferred_element_type=F32)


def dot3(left, right, dims=((1,), (0,))):
    left_hi, left_lo = left
    right_hi, right_lo = right
    return (
        dot(left_hi, right_lo, dims) + dot(left_lo, right_hi, dims) + dot(left_hi, right_hi, dims)
    )


def layer_norm(values, gain):
    center = values - jnp.mean(values, axis=-1, keepdims=True)
    spread = jnp.mean(center * center, axis=-1, keepdims=True)
    return center * lax.rsqrt(spread + 1e-05) * gain


def gelu(values):
    return 0.5 * values * (1.0 + lax.erf(values * 0.7071067811865476))


def block_kernel(
    sizes,
    *refs,
):
    inputs, out = refs[:11], refs[11]
    latent = inputs[0]
    (
        lat, w_small, w_large, gain_embed, gain_attn, w_qkv, pos_bias, w_proj, gain_mlp, w_up, w_down,
        eo_hi, eo_lo, oe_hi, oe_lo, wc, we, wo, wq, wp, wu, wd, bias,
        emb, recv, done, col_halo, col_edge,
        halo_send, halo_recv, go_send, go_recv, back_send, back_recv, load_sem, part_sem,
    ) = refs[12:]
    loaded = (
        None, w_small, w_large, gain_embed, gain_attn, w_qkv, pos_bias, w_proj, gain_mlp, w_up, w_down,
    )
    row_count, col_count, members, phases, groups = sizes
    rows, cols, chan = latent.shape
    tile_rows, tile_cols = rows // 2, cols // 2
    feat = gain_embed.shape[1]
    half = feat // 2
    quarter_rows, quarter_cols = tile_rows // 4, tile_cols // 4
    share = tile_rows * tile_cols // STAGES // members
    runs = share // groups
    tokens = members * groups
    head = feat // HEADS
    half_members = members // 2
    half_cols = col_count // 2
    per = members // col_count

    r = lax.axis_index("rows")
    c = lax.axis_index("cols")
    core = lax.rem(r, phases)
    side, spot = c // half_cols, lax.rem(c, half_cols)
    band = r // phases
    me = side * half_members + band * half_cols + spot

    def place(member):
        rest = lax.rem(member, half_members)
        return (
            (rest // half_cols) * phases + core,
            member // half_members * half_cols + lax.rem(rest, half_cols),
        )

    def other(step):
        crossing = step < half_members
        index = jnp.where(crossing, step, members - 1 - step)
        there = jnp.where(crossing, 1 - side, side)
        to_spot = lax.rem(spot + index // per, half_cols)
        to_band = lax.rem(band + lax.rem(index, per), per)
        return there * half_members + to_band * half_cols + to_spot

    first = 1 - side
    second = side
    first_row = quarter_rows * (1 + first)
    second_row = quarter_rows * (1 + second)
    left_col, right_col = 2 * quarter_cols - 8, 6 * quarter_cols + 8
    wide = right_col - left_col

    def piece(index, row, row_num, col, col_num):
        return pltpu.make_async_copy(
            latent.at[pl.ds(row, row_num), pl.ds(col, col_num)],
            lat.at[pl.ds(row + 1, row_num), pl.ds(col + 8, col_num)],
            part_sem.at[index],
        )

    second_line = 2 * second_row + 2 * second
    pieces = [
        piece(0, 2 * first_row - 1, 2 * quarter_rows + 2, left_col, wide),
        piece(1, 0, rows, 0, 8),
        piece(2, 0, rows, cols - 8, 8),
        piece(3, second_line - 1, 2 * quarter_rows, left_col, wide),
        piece(4, 0, 2 * quarter_rows - 1, left_col, wide),
        piece(5, 6 * quarter_rows + 1, 2 * quarter_rows - 1, left_col, wide),
        piece(6, 0, rows, 8, left_col - 8),
        piece(7, 0, rows, right_col, cols - 8 - right_col),
    ]

    def load(index):
        return pltpu.make_async_copy(inputs[index], loaded[index], load_sem.at[index])

    pieces[0].start()
    load(1).start()
    load(2).start()
    load(3).start()

    barrier = pltpu.get_barrier_semaphore()

    def greet(step, carry):
        pl.semaphore_signal(barrier, inc=1, device_id=place(other(step)), device_id_type=MESH)
        return carry

    lax.fori_loop(0, members - 1, greet, 0)
    up, down = r > 0, r < row_count - 1
    west, east = c > 0, c < col_count - 1
    for row_ok, dr in ((up, -1), (down, 1)):
        for col_ok, dc in ((True, 0), (west, -1), (east, 1)):
            ok = row_ok if col_ok is True else jnp.logical_and(row_ok, col_ok)

            @pl.when(ok)
            def _(dr=dr, dc=dc):
                pl.semaphore_signal(barrier, inc=1, device_id=(r + dr, c + dc), device_id_type=MESH)

    for index in range(1, 8):
        pieces[index].start()
    for index in range(4, 11):
        load(index).start()

    def keep(ref, index, values):
        ref[(0,) + index], ref[(1,) + index] = split(values)

    load(1).wait()
    load(2).wait()
    for p in range(2):
        keep(wc, (p, slice(None), slice(0, half)), w_small[2 * p * chan : 2 * (p + 1) * chan])
        start = (p + 1) * 4 * chan + chan
        keep(wc, (p, slice(None), slice(half, feat)), w_large[start : start + 2 * chan])
        start = 3 * p * 4 * chan + chan
        keep(we, (p,), w_large[start : start + 2 * chan])
    for p in range(4):
        keep(wo, (p, slice(0, chan)), w_large[4 * p * chan : (4 * p + 1) * chan])
        keep(wo, (p, slice(chan, 2 * chan)), w_large[(4 * p + 3) * chan : (4 * p + 4) * chan])

    pieces[1].wait()
    pieces[2].wait()
    col_edge[0] = lat[pl.ds(1, rows), 8, :]
    col_edge[1] = lat[pl.ds(1, rows), cols + 7, :]
    number = lambda flag: jnp.where(flag, 1, 0)
    vertical = number(up) + number(down)
    horizontal = 1 + number(west) + number(east)
    pl.semaphore_wait(barrier, members - 1 + vertical * horizontal)

    both = jnp.logical_and
    left_pad, right_pad = pl.ds(0, 8), pl.ds(cols + 8, 8)
    head_cols, tail_cols = pl.ds(0, 8), pl.ds(cols - 8, 8)
    middle = pl.ds(8, cols)
    plan = [
        (west, east, (r, c - 1), col_edge.at[0], col_halo.at[1]),
        (east, west, (r, c + 1), col_edge.at[1], col_halo.at[0]),
        (up, down, (r - 1, c), latent.at[0], lat.at[rows + 1, middle]),
        (down, up, (r + 1, c), latent.at[rows - 1], lat.at[0, middle]),
        (both(up, west), both(down, east), (r - 1, c - 1), latent.at[0, head_cols], lat.at[rows + 1, right_pad]),
        (both(up, east), both(down, west), (r - 1, c + 1), latent.at[0, tail_cols], lat.at[rows + 1, left_pad]),
        (both(down, west), both(up, east), (r + 1, c - 1), latent.at[rows - 1, head_cols], lat.at[0, right_pad]),
        (both(down, east), both(up, west), (r + 1, c + 1), latent.at[rows - 1, tail_cols], lat.at[0, left_pad]),
    ]

    def halo_copy(index):
        _, _, target, source, destination = plan[index]
        return pltpu.make_async_remote_copy(
            src_ref=source, dst_ref=destination, send_sem=halo_send.at[index],
            recv_sem=halo_recv.at[index], device_id=target, device_id_type=MESH,
        )

    for index in range(8):
        @pl.when(plan[index][0])
        def _(index=index):
            halo_copy(index).start()

    def build(start, stop, col, num):
        area = pl.ds(col, num)

        def line(t, carry):
            b, a = lax.rem(t, 2), t // 2
            for hi, lo, shifts in ((eo_hi, eo_lo, (0, 1)), (oe_hi, oe_lo, (-1, 2))):
                for place_at, shift in zip((slice(0, chan), slice(chan, 2 * chan)), shifts):
                    values = lat[t, pl.ds(8 + 2 * col + shift, num, stride=2), :]
                    hi[b, a, area, place_at], lo[b, a, area, place_at] = split(values)
            return carry

        lax.fori_loop(start, stop, line, 0)

    def go(s, member):
        return pltpu.make_async_remote_copy(
            src_ref=emb.at[s, member], dst_ref=recv.at[s, me], send_sem=go_send.at[s, member],
            recv_sem=go_recv.at[s, me], device_id=place(member), device_id_type=MESH,
        )

    def arrival(s, member):
        return pltpu.make_async_remote_copy(
            src_ref=emb.at[s, member], dst_ref=recv.at[s, member], send_sem=go_send.at[s, member],
            recv_sem=go_recv.at[s, member], device_id=place(member), device_id_type=MESH,
        )

    def embed(s, part, row, row_num, col, col_num):
        def taps(hi, lo, p):
            where = (p % 2, pl.ds(row + p // 2, row_num), pl.ds(col, col_num))
            return tuple(ref[where].reshape(row_num * col_num, 2 * chan) for ref in (hi, lo))

        def pair(ref, index):
            return ref[0, index], ref[1, index]

        wide = dot3(taps(eo_hi, eo_lo, 1), pair(wc, 0)) + dot3(taps(eo_hi, eo_lo, 2), pair(wc, 1))
        thin = dot3(taps(eo_hi, eo_lo, 0), pair(we, 0)) + dot3(taps(eo_hi, eo_lo, 3), pair(we, 1))
        for p in range(4):
            thin = thin + dot3(taps(oe_hi, oe_lo, p), pair(wo, p))
        joined = jnp.concatenate([wide[:, :half], wide[:, half:] + thin], axis=-1)
        emb[s, pl.ds(part * half_members, half_members)] = layer_norm(joined, gain_embed[...]).reshape(
            half_members, runs, groups, feat
        )

    def send_go(s, start, stop):
        def send(step, carry):
            go(s, other(step)).start()
            return carry

        lax.fori_loop(start, stop, send, 0)

    pieces[0].wait()
    load(3).wait()
    build(2 * first_row, 2 * first_row + 2 * quarter_rows + 2, quarter_cols, 2 * quarter_cols)
    embed(0, first, first_row, quarter_rows, quarter_cols, 2 * quarter_cols)
    send_go(0, 0, half_members)
    pieces[3].wait()
    build(second_line, second_line + 2 * quarter_rows, quarter_cols, 2 * quarter_cols)
    embed(0, second, second_row, quarter_rows, quarter_cols, 2 * quarter_cols)
    send_go(0, half_members, members - 1)
    recv[0, me] = emb[0, me]

    for index in range(8):
        _, arrives, _, _, destination = plan[index]

        @pl.when(arrives)
        def _(index=index):
            halo_copy(index).wait_recv()

        @pl.when(jnp.logical_not(arrives))
        def _(destination=destination):
            destination[...] = jnp.zeros(destination.shape, F32)

    for index in range(4, 8):
        pieces[index].wait()

    def edge(t, carry):
        lat[t + 1, pl.ds(7, 1)] = col_halo[0, pl.ds(t, 1)]
        lat[t + 1, pl.ds(cols + 8, 1)] = col_halo[1, pl.ds(t, 1)]
        return carry

    lax.fori_loop(0, rows, edge, 0)

    build(0, 2 * quarter_rows, quarter_cols, 2 * quarter_cols)
    build(6 * quarter_rows + 2, rows + 2, quarter_cols, 2 * quarter_cols)
    for part in range(2):
        embed(1, part, 3 * quarter_rows * part, quarter_rows, quarter_cols, 2 * quarter_cols)
    send_go(1, 0, members - 1)
    recv[1, me] = emb[1, me]
    for s, col in ((2, 0), (3, 3 * quarter_cols)):
        build(0, rows + 2, col, quarter_cols)
        for part in range(2):
            embed(s, part, 2 * quarter_rows * part, 2 * quarter_rows, col, quarter_cols)
        send_go(s, 0, members - 1)
        recv[s, me] = emb[s, me]

    for index in range(4, 11):
        load(index).wait()

    for ref, source in ((wq, w_qkv), (wp, w_proj), (wu, w_up), (wd, w_down)):
        ref[0], ref[1] = split(source[...])

    slot = lax.broadcasted_iota(jnp.int32, (tokens, members), 0) // groups
    rest = lax.rem(slot, half_members)
    number_of = (rest // half_cols) * col_count + (slot // half_members) * half_cols + lax.rem(rest, half_cols)
    spread = (number_of == lax.broadcasted_iota(jnp.int32, (tokens, members), 1)).astype(F32)
    same = lax.rem(lax.broadcasted_iota(jnp.int32, (tokens, tokens), 0), groups) == lax.rem(
        lax.broadcasted_iota(jnp.int32, (tokens, tokens), 1), groups
    )
    exact = functools.partial(
        lax.dot_general, precision=lax.Precision.HIGHEST, preferred_element_type=F32
    )

    def widen(h, carry):
        tall = exact(spread, pos_bias[h], (((1,), (0,)), ((), ())))
        bias[h] = jnp.where(same, exact(tall, spread, (((1,), (1,)), ((), ()))), -1e30)
        return carry

    lax.fori_loop(0, HEADS, widen, 0)

    def home(s, owner, across):
        start = owner * share
        if across:
            line = start // (2 * quarter_cols)
            column = quarter_cols + lax.rem(start, 2 * quarter_cols)
            row = jnp.where(
                s == 0,
                line + quarter_rows,
                jnp.where(line < quarter_rows, line, line + 2 * quarter_rows),
            )
            return out.at[row, pl.ds(column // groups, runs)]
        row = start // quarter_cols
        column = jnp.where(s == 2, 0, 3 * quarter_cols) + lax.rem(start, quarter_cols)
        if share > quarter_cols:
            return out.at[pl.ds(row, runs), column // groups]
        return out.at[row, pl.ds(column // groups, runs)]

    def back(s, member, across):
        return pltpu.make_async_remote_copy(
            src_ref=done.at[s, member], dst_ref=home(s, me, across), send_sem=back_send.at[s, member],
            recv_sem=back_recv.at[s, me], device_id=place(member), device_id_type=MESH,
        )

    def back_arrival(s, owner, across):
        return pltpu.make_async_remote_copy(
            src_ref=done.at[s, owner], dst_ref=home(s, owner, across), send_sem=back_send.at[s, owner],
            recv_sem=back_recv.at[s, owner], device_id=place(owner), device_id_type=MESH,
        )

    def own(s, across):
        return pltpu.make_async_copy(done.at[s, me], home(s, me, across), back_recv.at[s, me])

    lane_head = lax.broadcasted_iota(jnp.int32, (1, feat), 1) // head
    scale = 1.0 / (head**0.5)

    def block(s, b):
        x = recv[s, :, b].reshape(tokens, feat)
        normed = split(layer_norm(x, gain_attn[...]))
        qkv = dot3(normed, (wq[0], wq[1]))
        q = qkv[:, :feat] * scale
        k = split(qkv[:, feat : 2 * feat])
        v = split(qkv[:, 2 * feat :])
        mixed = jnp.zeros((tokens, feat), F32)
        for h in range(HEADS):
            mine = lane_head == h
            scores = dot3(split(jnp.where(mine, q, 0.0)), k, ((1,), (1,))) + bias[h]
            expd = jnp.exp(scores - jnp.max(scores, axis=-1, keepdims=True))
            total = jnp.sum(expd, axis=-1, keepdims=True)
            mixed = mixed + jnp.where(mine, dot3(split(expd), v) / total, 0.0)
        after = x + dot3(split(mixed), (wp[0], wp[1]))
        hidden = gelu(dot3(split(layer_norm(after, gain_mlp[...])), (wu[0], wu[1])))
        result = after + dot3(split(hidden), (wd[0], wd[1]))
        done[s, :, b] = result.reshape(members, groups, feat)

    def process(s, carry):
        def await_one(step, inner):
            arrival(s, other(step)).wait_recv()
            return inner

        lax.fori_loop(0, members - 1, await_one, 0)

        def work(b, inner):
            block(s, b)
            return inner

        lax.fori_loop(0, runs, work, 0)

        for across, mine in ((True, s < 2), (False, s >= 2)):
            @pl.when(mine)
            def _(across=across):
                def send(step, inner):
                    back(s, other(step), across).start()
                    return inner

                lax.fori_loop(0, members - 1, send, 0)
                own(s, across).start()

        return carry

    lax.fori_loop(0, STAGES, process, 0)

    for s in range(STAGES):
        def sent(step, carry, s=s):
            member = other(step)
            go(s, member).wait_send()
            back(s, member, s < 2).wait_send()
            return carry

        lax.fori_loop(0, members - 1, sent, 0)
    for index in range(8):
        @pl.when(plan[index][0])
        def _(index=index):
            halo_copy(index).wait_send()
    for s in range(STAGES):
        def landed(step, carry, s=s):
            back_arrival(s, other(step), s < 2).wait_recv()
            return carry

        lax.fori_loop(0, members - 1, landed, 0)
        own(s, s < 2).wait()


def per_device(
    latent, w_small, w_large, gain_embed, gain_attn, w_qkv, pos_bias, w_proj, gain_mlp, w_up, w_down
):
    row_count = lax.axis_size("rows")
    col_count = lax.axis_size("cols")
    samples, rows, cols, chan = latent.shape
    tile_rows, tile_cols = rows // 2, cols // 2
    feat = gain_embed.shape[0]
    half = feat // 2
    members = pos_bias.shape[1]
    phases = row_count // (members // col_count)
    share = tile_rows * tile_cols // STAGES // members
    groups = max(8, min(share, 256 // members))
    tokens = members * groups
    pixels = pltpu.VMEM((2, tile_rows + 1, tile_cols, 2 * chan), BF16)
    exchange = pltpu.VMEM((STAGES, members, share // groups, groups, feat), F32)
    dma = pltpu.SemaphoreType.DMA
    inputs = (
        latent[0], w_small, w_large, gain_embed[None], gain_attn[None], w_qkv, pos_bias, w_proj,
        gain_mlp[None], w_up, w_down,
    )
    halves = lambda *shape: pltpu.VMEM((2,) + shape, BF16)
    out_bytes = tile_rows * tile_cols * feat * 4
    out = pl.pallas_call(
        functools.partial(block_kernel, (row_count, col_count, members, phases, groups)),
        name="crossformer_block",
        out_shape=pltpu.VMEM((tile_rows, tile_cols // groups, groups, feat), F32),
        in_specs=[pl.BlockSpec(memory_space=pltpu.HBM)] * 11,
        out_specs=pl.BlockSpec(memory_space=pltpu.VMEM),
        scratch_shapes=[pltpu.VMEM((rows + 2, cols + 16, chan), F32)]
        + [pltpu.VMEM(array.shape, F32) for array in inputs[1:]]
        + [
            pixels, pixels, pixels, pixels,
            halves(2, 2 * chan, feat),
            halves(2, 2 * chan, half),
            halves(4, 2 * chan, half),
            halves(*w_qkv.shape),
            halves(*w_proj.shape),
            halves(*w_up.shape),
            halves(*w_down.shape),
            pltpu.VMEM((HEADS, tokens, tokens), F32),
            exchange, exchange, exchange,
            pltpu.VMEM((2, rows, chan), F32),
            pltpu.VMEM((2, rows, chan), F32),
            dma((8,)), dma((8,)),
            dma((STAGES, members)), dma((STAGES, members)),
            dma((STAGES, members)), dma((STAGES, members)),
            dma((11,)), dma((8,)),
        ],
        compiler_params=pltpu.CompilerParams(
            collective_id=0, has_side_effects=True, vmem_limit_bytes=67043328 - out_bytes
        ),
    )(*inputs)
    return out.reshape(samples, tile_rows, tile_cols, feat)


def solution(mesh):
    in_specs = (P(None, "rows", "cols", None),) + (P(),) * 10
    out_specs = P(None, "rows", "cols", None)
    return jax.shard_map(
        per_device, mesh=mesh, in_specs=in_specs, out_specs=out_specs, check_vma=False
    )
```

```python
import functools

import jax
import jax.numpy as jnp
from jax import lax
from jax.experimental import pallas as pl
from jax.experimental.pallas import tpu as pltpu
from jax.sharding import PartitionSpec as P

HEADS = 8
STAGES = 2
PARTS = 2
MESH = pl.DeviceIdType.MESH
F32 = jnp.float32
BF16 = jnp.bfloat16


def split(values):
    high = values.astype(BF16)
    return high, (values - high.astype(F32)).astype(BF16)


def dot(left, right, dims=((1,), (0,))):
    return lax.dot_general(left, right, (dims, ((), ())), preferred_element_type=F32)


def dot3(left, right, dims=((1,), (0,))):
    left_hi, left_lo = left
    right_hi, right_lo = right
    return (
        dot(left_hi, right_lo, dims) + dot(left_lo, right_hi, dims) + dot(left_hi, right_hi, dims)
    )


def layer_norm(values, gain):
    center = values - jnp.mean(values, axis=-1, keepdims=True)
    spread = jnp.mean(center * center, axis=-1, keepdims=True)
    return center * lax.rsqrt(spread + 1e-05) * gain


def gelu(values):
    return 0.5 * values * (1.0 + lax.erf(values * 0.7071067811865476))


def block_kernel(
    sizes,
    *refs,
):
    inputs, out = refs[:11], refs[11]
    latent = inputs[0]
    (
        lat, w_small, w_large, gain_embed, gain_attn, w_qkv, pos_bias, w_proj, gain_mlp, w_up, w_down,
        eo_hi, eo_lo, oe_hi, oe_lo, wc, we, wo, wq, wp, wu, wd, bias,
        emb, recv, done, col_halo, col_edge,
        halo_send, halo_recv, go_send, go_recv, back_send, back_recv, load_sem, part_sem,
    ) = refs[12:]
    loaded = (
        None, w_small, w_large, gain_embed, gain_attn, w_qkv, pos_bias, w_proj, gain_mlp, w_up, w_down,
    )
    row_count, col_count, members, phases, groups = sizes
    rows, cols, chan = latent.shape
    tile_rows, tile_cols = rows // 2, cols // 2
    feat = gain_embed.shape[1]
    half = feat // 2
    quarter_cols = tile_cols // 4
    share = tile_rows * tile_cols // STAGES // members
    lines = max(1, share // (2 * quarter_cols))
    runs = share // groups // lines
    tokens = members * groups
    head = feat // HEADS
    half_members = members // 2
    half_cols = col_count // 2
    per = members // col_count
    strip = tile_rows // 4

    r = lax.axis_index("rows")
    c = lax.axis_index("cols")
    core = lax.rem(r, phases)
    side, spot = c // half_cols, lax.rem(c, half_cols)
    band = r // phases
    me = side * half_members + spot * per + band

    def place(member):
        return (
            lax.rem(member, per) * phases + core,
            member // half_members * half_cols + lax.rem(member, half_members) // per,
        )

    def other(step):
        crossing = step < half_members
        index = jnp.where(crossing, step, members - 1 - step)
        there = jnp.where(crossing, 1 - side, side)
        to_spot = lax.rem(spot + index // per, half_cols)
        to_band = lax.rem(band + lax.rem(index, per), per)
        return there * half_members + to_spot * per + to_band

    first, fourth = 2 - side, 3 * side
    second, third = 3 - fourth, 3 - first
    left_col, right_col = 2 * quarter_cols - 8, 6 * quarter_cols + 8
    wide = right_col - left_col
    strip_lines = 2 * strip
    third_line = strip_lines * third + 2 * side

    def piece(index, row, row_num, col, col_num):
        return pltpu.make_async_copy(
            latent.at[pl.ds(row, row_num), pl.ds(col, col_num)],
            lat.at[pl.ds(row + 1, row_num), pl.ds(col + 8, col_num)],
            part_sem.at[index],
        )

    pieces = [
        piece(0, strip_lines * first - 1, strip_lines + 2, left_col, wide),
        piece(1, 0, rows, 0, 8),
        piece(2, 0, rows, cols - 8, 8),
        piece(3, third_line - 1, strip_lines, left_col, wide),
        piece(4, 0, strip_lines - 1, left_col, wide),
        piece(5, 3 * strip_lines + 1, strip_lines - 1, left_col, wide),
        piece(6, 0, rows, 8, left_col - 8),
        piece(7, 0, rows, right_col, cols - 8 - right_col),
    ]

    def load(index):
        return pltpu.make_async_copy(inputs[index], loaded[index], load_sem.at[index])

    pieces[0].start()
    load(1).start()
    load(2).start()
    load(3).start()

    barrier = pltpu.get_barrier_semaphore()

    def greet(step, carry):
        pl.semaphore_signal(barrier, inc=1, device_id=place(other(step)), device_id_type=MESH)
        return carry

    lax.fori_loop(0, members - 1, greet, 0)
    up, down = r > 0, r < row_count - 1
    west, east = c > 0, c < col_count - 1
    for row_ok, dr in ((up, -1), (down, 1)):
        for col_ok, dc in ((True, 0), (west, -1), (east, 1)):
            ok = row_ok if col_ok is True else jnp.logical_and(row_ok, col_ok)

            @pl.when(ok)
            def _(dr=dr, dc=dc):
                pl.semaphore_signal(barrier, inc=1, device_id=(r + dr, c + dc), device_id_type=MESH)

    for index in range(1, 8):
        pieces[index].start()
    for index in range(4, 11):
        load(index).start()

    def keep(ref, index, values):
        ref[(0,) + index], ref[(1,) + index] = split(values)

    load(1).wait()
    load(2).wait()
    for p in range(2):
        keep(wc, (p, slice(None), slice(0, half)), w_small[2 * p * chan : 2 * (p + 1) * chan])
        start = (p + 1) * 4 * chan + chan
        keep(wc, (p, slice(None), slice(half, feat)), w_large[start : start + 2 * chan])
        start = 3 * p * 4 * chan + chan
        keep(we, (p,), w_large[start : start + 2 * chan])
    for p in range(4):
        keep(wo, (p, slice(0, chan)), w_large[4 * p * chan : (4 * p + 1) * chan])
        keep(wo, (p, slice(chan, 2 * chan)), w_large[(4 * p + 3) * chan : (4 * p + 4) * chan])

    def build(start, stop, col, num):
        area = pl.ds(col, num)

        def line(t, carry):
            b, a = lax.rem(t, 2), t // 2
            for hi, lo, shifts in ((eo_hi, eo_lo, (0, 1)), (oe_hi, oe_lo, (-1, 2))):
                for place_at, shift in zip((slice(0, chan), slice(chan, 2 * chan)), shifts):
                    values = lat[t, pl.ds(8 + 2 * col + shift, num, stride=2), :]
                    hi[b, a, area, place_at], lo[b, a, area, place_at] = split(values)
            return carry

        lax.fori_loop(start, stop, line, 0)

    def go(s, member):
        return pltpu.make_async_remote_copy(
            src_ref=emb.at[s, member], dst_ref=recv.at[s, me], send_sem=go_send.at[s, member],
            recv_sem=go_recv.at[s, me], device_id=place(member), device_id_type=MESH,
        )

    def arrival(s, member):
        return pltpu.make_async_remote_copy(
            src_ref=emb.at[s, member], dst_ref=recv.at[s, member], send_sem=go_send.at[s, member],
            recv_sem=go_recv.at[s, member], device_id=place(member), device_id_type=MESH,
        )

    def embed(s, part, row, row_num, col, col_num):
        def taps(hi, lo, p):
            where = (p % 2, pl.ds(row + p // 2, row_num), pl.ds(col, col_num))
            return tuple(ref[where].reshape(row_num * col_num, 2 * chan) for ref in (hi, lo))

        def pair(ref, index):
            return ref[0, index], ref[1, index]

        wide = dot3(taps(eo_hi, eo_lo, 1), pair(wc, 0)) + dot3(taps(eo_hi, eo_lo, 2), pair(wc, 1))
        thin = dot3(taps(eo_hi, eo_lo, 0), pair(we, 0)) + dot3(taps(eo_hi, eo_lo, 3), pair(we, 1))
        for p in range(4):
            thin = thin + dot3(taps(oe_hi, oe_lo, p), pair(wo, p))
        joined = jnp.concatenate([wide[:, :half], wide[:, half:] + thin], axis=-1)
        emb[s, pl.ds(part * (members // 4), members // 4)] = layer_norm(joined, gain_embed[...]).reshape(
            members // 4, lines, runs, groups, feat
        )

    def send_go(s, part):
        def send(step, carry):
            member = part * (members // 4) + lax.rem(me + step, members // 4)

            @pl.when(member != me)
            def _():
                go(s, member).start()

            return carry

        lax.fori_loop(0, members // 4, send, 0)

    pieces[0].wait()
    load(3).wait()
    def center(part):
        embed(0, part, strip * part, strip, quarter_cols, 2 * quarter_cols)

    build(strip_lines * first, strip_lines * first + strip_lines + 2, quarter_cols, 2 * quarter_cols)
    center(first)
    pieces[1].wait()
    pieces[2].wait()
    col_edge[0] = lat[pl.ds(1, rows), 8, :]
    col_edge[1] = lat[pl.ds(1, rows), cols + 7, :]
    number = lambda flag: jnp.where(flag, 1, 0)
    vertical = number(up) + number(down)
    horizontal = 1 + number(west) + number(east)
    pl.semaphore_wait(barrier, members - 1 + vertical * horizontal)

    both = jnp.logical_and
    left_pad, right_pad = pl.ds(0, 8), pl.ds(cols + 8, 8)
    head_cols, tail_cols = pl.ds(0, 8), pl.ds(cols - 8, 8)
    middle = pl.ds(8, cols)
    plan = [
        (west, east, (r, c - 1), col_edge.at[0], col_halo.at[1]),
        (east, west, (r, c + 1), col_edge.at[1], col_halo.at[0]),
        (up, down, (r - 1, c), latent.at[0], lat.at[rows + 1, middle]),
        (down, up, (r + 1, c), latent.at[rows - 1], lat.at[0, middle]),
        (both(up, west), both(down, east), (r - 1, c - 1), latent.at[0, head_cols], lat.at[rows + 1, right_pad]),
        (both(up, east), both(down, west), (r - 1, c + 1), latent.at[0, tail_cols], lat.at[rows + 1, left_pad]),
        (both(down, west), both(up, east), (r + 1, c - 1), latent.at[rows - 1, head_cols], lat.at[0, right_pad]),
        (both(down, east), both(up, west), (r + 1, c + 1), latent.at[rows - 1, tail_cols], lat.at[0, left_pad]),
    ]

    def halo_copy(index):
        _, _, target, source, destination = plan[index]
        return pltpu.make_async_remote_copy(
            src_ref=source, dst_ref=destination, send_sem=halo_send.at[index],
            recv_sem=halo_recv.at[index], device_id=target, device_id_type=MESH,
        )

    def send_halo(indices):
        for index in indices:
            @pl.when(plan[index][0])
            def _(index=index):
                halo_copy(index).start()

    send_halo(range(8))
    send_go(0, first)

    def await_halo(indices):
        for index in indices:
            _, arrives, _, _, destination = plan[index]

            @pl.when(arrives)
            def _(index=index):
                halo_copy(index).wait_recv()

            @pl.when(jnp.logical_not(arrives))
            def _(destination=destination):
                destination[...] = jnp.zeros(destination.shape, F32)

    pieces[4].wait()
    pieces[5].wait()
    await_halo((2, 3))
    outer = 3 * strip_lines + 2
    build(outer * (1 - side), outer * (1 - side) + strip_lines, quarter_cols, 2 * quarter_cols)
    center(second)
    send_go(0, second)
    pieces[3].wait()
    build(third_line, third_line + strip_lines, quarter_cols, 2 * quarter_cols)
    center(third)
    send_go(0, third)
    build(outer * side, outer * side + strip_lines, quarter_cols, 2 * quarter_cols)
    center(fourth)
    send_go(0, fourth)
    recv[0, me] = emb[0, me]

    await_halo((0, 1, 4, 5, 6, 7))
    pieces[6].wait()
    pieces[7].wait()

    def edge(t, carry):
        lat[t + 1, pl.ds(7, 1)] = col_halo[0, pl.ds(t, 1)]
        lat[t + 1, pl.ds(cols + 8, 1)] = col_halo[1, pl.ds(t, 1)]
        return carry

    lax.fori_loop(0, rows, edge, 0)

    def outside(step, carry):
        part = lax.rem(2 * (1 - side) + step, 4)
        low = lax.rem(part, 2)
        col = pl.multiple_of(part // 2 * (3 * quarter_cols), quarter_cols)
        line = 4 * strip * low
        build(line, line + 4 * strip + 2, col, quarter_cols)
        embed(1, part, 2 * strip * low, 2 * strip, col, quarter_cols)
        send_go(1, part)
        return carry

    lax.fori_loop(0, 4, outside, 0)
    recv[1, me] = emb[1, me]

    for index in range(4, 11):
        load(index).wait()

    for ref, source in ((wq, w_qkv), (wp, w_proj), (wu, w_up), (wd, w_down)):
        ref[0], ref[1] = split(source[...])

    slot = lax.broadcasted_iota(jnp.int32, (tokens, members), 0) // groups
    number_of = lax.rem(slot, per) * col_count + slot // per
    spread = (number_of == lax.broadcasted_iota(jnp.int32, (tokens, members), 1)).astype(F32)
    same = lax.rem(lax.broadcasted_iota(jnp.int32, (tokens, tokens), 0), groups) == lax.rem(
        lax.broadcasted_iota(jnp.int32, (tokens, tokens), 1), groups
    )
    exact = functools.partial(
        lax.dot_general, precision=lax.Precision.HIGHEST, preferred_element_type=F32
    )

    def widen(h, carry):
        tall = exact(spread, pos_bias[h], (((1,), (0,)), ((), ())))
        bias[h] = jnp.where(same, exact(tall, spread, (((1,), (1,)), ((), ()))), -1e30)
        return carry

    lax.fori_loop(0, HEADS, widen, 0)

    whole = PARTS == 1 or lines == 1
    splits = 1 if whole else lines

    def home(s, owner, part):
        start = owner * share
        if s == 0:
            place_at = out.at[start // (2 * quarter_cols * lines)]
            column = (quarter_cols + lax.rem(start, 2 * quarter_cols)) // groups
            return place_at.at[:, pl.ds(column, runs)] if whole else place_at.at[part, pl.ds(column, runs)]
        row = lax.rem(start, tile_rows * quarter_cols) // quarter_cols
        column = (start // (tile_rows * quarter_cols) * (3 * quarter_cols) + lax.rem(start, quarter_cols)) // groups
        if share <= quarter_cols:
            return out.at[row, :, pl.ds(column, runs)]
        if whole:
            return out.at[pl.ds(row // lines, runs), :, column]
        return out.at[row // lines + part, :, column]

    def ready(s, member, part):
        return done.at[s, member] if whole else done.at[s, member, part]

    def back(s, member, part):
        return pltpu.make_async_remote_copy(
            src_ref=ready(s, member, part), dst_ref=home(s, me, part), send_sem=back_send.at[s, part, member],
            recv_sem=back_recv.at[s, part, me], device_id=place(member), device_id_type=MESH,
        )

    def back_arrival(s, owner, part):
        return pltpu.make_async_remote_copy(
            src_ref=ready(s, owner, part), dst_ref=home(s, owner, part), send_sem=back_send.at[s, part, owner],
            recv_sem=back_recv.at[s, part, owner], device_id=place(owner), device_id_type=MESH,
        )

    def own(s, part):
        return pltpu.make_async_copy(ready(s, me, part), home(s, me, part), back_recv.at[s, part, me])

    lane_head = lax.broadcasted_iota(jnp.int32, (1, feat), 1) // head
    scale = 1.0 / (head**0.5)

    def block(s, b):
        where = (s, slice(None), b // runs, lax.rem(b, runs))
        x = recv[where].reshape(tokens, feat)
        normed = split(layer_norm(x, gain_attn[...]))
        qkv = dot3(normed, (wq[0], wq[1]))
        q = qkv[:, :feat] * scale
        k = split(qkv[:, feat : 2 * feat])
        v = split(qkv[:, 2 * feat :])
        mixed = jnp.zeros((tokens, feat), F32)
        for h in range(HEADS):
            mine = lane_head == h
            scores = dot3(split(jnp.where(mine, q, 0.0)), k, ((1,), (1,))) + bias[h]
            expd = jnp.exp(scores - jnp.max(scores, axis=-1, keepdims=True))
            total = jnp.sum(expd, axis=-1, keepdims=True)
            mixed = mixed + jnp.where(mine, dot3(split(expd), v) / total, 0.0)
        after = x + dot3(split(mixed), (wp[0], wp[1]))
        hidden = gelu(dot3(split(layer_norm(after, gain_mlp[...])), (wu[0], wu[1])))
        result = after + dot3(split(hidden), (wd[0], wd[1]))
        done[where] = result.reshape(members, groups, feat)

    def process(s, carry):
        def await_one(step, inner):
            arrival(s, other(step)).wait_recv()
            return inner

        lax.fori_loop(0, members - 1, await_one, 0)

        def some(part, inner):
            def work(b, inside):
                block(s, b)
                return inside

            count = lines * runs // splits
            lax.fori_loop(part * count, part * count + count, work, 0)

            for stage in range(STAGES):
                @pl.when(s == stage)
                def _(stage=stage):
                    def send(step, inside):
                        back(stage, other(step), part).start()
                        return inside

                    lax.fori_loop(0, members - 1, send, 0)
                    own(stage, part).start()

            return inner

        lax.fori_loop(0, splits, some, 0)
        return carry

    lax.fori_loop(0, STAGES, process, 0)

    for s in range(STAGES):
        def sent(step, carry, s=s):
            member = other(step)
            go(s, member).wait_send()
            for part in range(splits):
                back(s, member, part).wait_send()
            return carry

        lax.fori_loop(0, members - 1, sent, 0)
    for index in range(8):
        @pl.when(plan[index][0])
        def _(index=index):
            halo_copy(index).wait_send()
    for s in range(STAGES):
        def landed(step, carry, s=s):
            for part in range(splits):
                back_arrival(s, other(step), part).wait_recv()
            return carry

        lax.fori_loop(0, members - 1, landed, 0)
        for part in range(splits):
            own(s, part).wait()


def per_device(
    latent, w_small, w_large, gain_embed, gain_attn, w_qkv, pos_bias, w_proj, gain_mlp, w_up, w_down
):
    row_count = lax.axis_size("rows")
    col_count = lax.axis_size("cols")
    samples, rows, cols, chan = latent.shape
    tile_rows, tile_cols = rows // 2, cols // 2
    feat = gain_embed.shape[0]
    half = feat // 2
    members = pos_bias.shape[1]
    phases = row_count // (members // col_count)
    share = tile_rows * tile_cols // STAGES // members
    groups = max(8, min(share, 256 // members))
    tokens = members * groups
    pixels = pltpu.VMEM((2, tile_rows + 1, tile_cols, 2 * chan), BF16)
    lines = max(1, share // (tile_cols // 2))
    exchange = pltpu.VMEM((STAGES, members, lines, share // groups // lines, groups, feat), F32)
    dma = pltpu.SemaphoreType.DMA
    inputs = (
        latent[0], w_small, w_large, gain_embed[None], gain_attn[None], w_qkv, pos_bias, w_proj,
        gain_mlp[None], w_up, w_down,
    )
    halves = lambda *shape: pltpu.VMEM((2,) + shape, BF16)
    out_bytes = tile_rows * tile_cols * feat * 4
    out = pl.pallas_call(
        functools.partial(block_kernel, (row_count, col_count, members, phases, groups)),
        name="crossformer_block",
        out_shape=pltpu.VMEM((tile_rows // lines, lines, tile_cols // groups, groups, feat), F32),
        in_specs=[pl.BlockSpec(memory_space=pltpu.HBM)] * 11,
        out_specs=pl.BlockSpec(memory_space=pltpu.VMEM),
        scratch_shapes=[pltpu.VMEM((rows + 2, cols + 16, chan), F32)]
        + [pltpu.VMEM(array.shape, F32) for array in inputs[1:]]
        + [
            pixels, pixels, pixels, pixels,
            halves(2, 2 * chan, feat),
            halves(2, 2 * chan, half),
            halves(4, 2 * chan, half),
            halves(*w_qkv.shape),
            halves(*w_proj.shape),
            halves(*w_up.shape),
            halves(*w_down.shape),
            pltpu.VMEM((HEADS, tokens, tokens), F32),
            exchange, exchange, exchange,
            pltpu.VMEM((2, rows, chan), F32),
            pltpu.VMEM((2, rows, chan), F32),
            dma((8,)), dma((8,)),
            dma((STAGES, members)), dma((STAGES, members)),
            dma((STAGES, lines, members)), dma((STAGES, lines, members)),
            dma((11,)), dma((8,)),
        ],
        compiler_params=pltpu.CompilerParams(
            collective_id=0, has_side_effects=True, vmem_limit_bytes=67043328 - out_bytes
        ),
    )(*inputs)
    return out.reshape(samples, tile_rows, tile_cols, feat)


def solution(mesh):
    in_specs = (P(None, "rows", "cols", None),) + (P(),) * 10
    out_specs = P(None, "rows", "cols", None)
    return jax.shard_map(
        per_device, mesh=mesh, in_specs=in_specs, out_specs=out_specs, check_vma=False
    )
```

```python
import functools

import jax
import jax.numpy as jnp
from jax import lax
from jax.experimental import pallas as pl
from jax.experimental.pallas import tpu as pltpu
from jax.sharding import PartitionSpec as P

HEADS = 8
STAGES = 2
PARTS = 2
LANES = 8
MESH = pl.DeviceIdType.MESH
F32 = jnp.float32
BF16 = jnp.bfloat16


def split(values):
    high = values.astype(BF16)
    return high, (values - high.astype(F32)).astype(BF16)


def dot(left, right, dims=((1,), (0,))):
    return lax.dot_general(left, right, (dims, ((), ())), preferred_element_type=F32)


def dot3(left, right, dims=((1,), (0,))):
    left_hi, left_lo = left
    right_hi, right_lo = right
    return (
        dot(left_hi, right_lo, dims) + dot(left_lo, right_hi, dims) + dot(left_hi, right_hi, dims)
    )


def layer_norm(values, gain):
    center = values - jnp.mean(values, axis=-1, keepdims=True)
    spread = jnp.mean(center * center, axis=-1, keepdims=True)
    return center * lax.rsqrt(spread + 1e-05) * gain


def gelu(values):
    return 0.5 * values * (1.0 + lax.erf(values * 0.7071067811865476))


def block_kernel(
    sizes,
    *refs,
):
    inputs, out = refs[:11], refs[11]
    latent = inputs[0]
    (
        lat, w_small, w_large, gain_embed, gain_attn, w_qkv, pos_bias, w_proj, gain_mlp, w_up, w_down,
        eo_hi, eo_lo, oe_hi, oe_lo, wc, we, wo, wq, wp, wu, wd, bias,
        emb, recv, done, col_halo, col_edge,
        halo_send, halo_recv, go_send, go_recv, back_send, back_recv, load_sem, part_sem,
    ) = refs[12:]
    loaded = (
        None, w_small, w_large, gain_embed, gain_attn, w_qkv, pos_bias, w_proj, gain_mlp, w_up, w_down,
    )
    row_count, col_count, members, phases, groups = sizes
    rows, cols, chan = latent.shape
    tile_rows, tile_cols = rows // 2, cols // 2
    feat = gain_embed.shape[1]
    half = feat // 2
    quarter_cols = tile_cols // 4
    share = tile_rows * tile_cols // STAGES // members
    lines = max(1, share // (2 * quarter_cols))
    runs = share // groups // lines
    tokens = members * groups
    head = feat // HEADS
    nest = members * LANES
    lane = min(feat, 128)
    pack = min(lane // head, max(1, 1024 // nest))
    half_members = members // 2
    half_cols = col_count // 2
    per = members // col_count
    strip = tile_rows // 4

    r = lax.axis_index("rows")
    c = lax.axis_index("cols")
    core = lax.rem(r, phases)
    side, spot = c // half_cols, lax.rem(c, half_cols)
    band = r // phases
    me = side * half_members + spot * per + band

    def place(member):
        return (
            lax.rem(member, per) * phases + core,
            member // half_members * half_cols + lax.rem(member, half_members) // per,
        )

    def other(step):
        group = step // per
        shift = col_count // 2 + (group + 1) // 2 * (2 * lax.rem(group, 2) - 1)
        to_col = lax.rem(c + shift + col_count, col_count)
        return to_col * per + lax.rem(band + step + 1, per)

    first, fourth = 2 - side, 3 * side
    second, third = 3 - fourth, 3 - first
    left_col, right_col = 2 * quarter_cols - 8, 6 * quarter_cols + 8
    wide = right_col - left_col
    strip_lines = 2 * strip
    third_line = strip_lines * third + 2 * side

    def piece(index, row, row_num, col, col_num):
        return pltpu.make_async_copy(
            latent.at[pl.ds(row, row_num), pl.ds(col, col_num)],
            lat.at[pl.ds(row + 1, row_num), pl.ds(col + 8, col_num)],
            part_sem.at[index],
        )

    pieces = [
        piece(0, strip_lines * first - 1, strip_lines + 2, left_col, wide),
        piece(1, 0, rows, 0, 8),
        piece(2, 0, rows, cols - 8, 8),
        piece(3, third_line - 1, strip_lines, left_col, wide),
        piece(4, 0, strip_lines - 1, left_col, wide),
        piece(5, 3 * strip_lines + 1, strip_lines - 1, left_col, wide),
        piece(6, 0, rows, 8, left_col - 8),
        piece(7, 0, rows, right_col, cols - 8 - right_col),
    ]

    def load(index):
        return pltpu.make_async_copy(inputs[index], loaded[index], load_sem.at[index])

    pieces[0].start()
    load(1).start()
    load(2).start()
    load(3).start()

    barrier = pltpu.get_barrier_semaphore()

    def greet(step, carry):
        pl.semaphore_signal(barrier, inc=1, device_id=place(other(step)), device_id_type=MESH)
        return carry

    lax.fori_loop(0, members - 1, greet, 0)
    up, down = r > 0, r < row_count - 1
    west, east = c > 0, c < col_count - 1
    for row_ok, dr in ((up, -1), (down, 1)):
        for col_ok, dc in ((True, 0), (west, -1), (east, 1)):
            ok = row_ok if col_ok is True else jnp.logical_and(row_ok, col_ok)

            @pl.when(ok)
            def _(dr=dr, dc=dc):
                pl.semaphore_signal(barrier, inc=1, device_id=(r + dr, c + dc), device_id_type=MESH)

    for index in range(1, 8):
        pieces[index].start()
    for index in range(4, 11):
        load(index).start()

    def keep(ref, index, values):
        ref[(0,) + index], ref[(1,) + index] = split(values)

    load(1).wait()
    load(2).wait()
    for p in range(2):
        keep(wc, (p, slice(None), slice(0, half)), w_small[2 * p * chan : 2 * (p + 1) * chan])
        start = (p + 1) * 4 * chan + chan
        keep(wc, (p, slice(None), slice(half, feat)), w_large[start : start + 2 * chan])
        start = 3 * p * 4 * chan + chan
        keep(we, (p,), w_large[start : start + 2 * chan])
    for p in range(4):
        keep(wo, (p, slice(0, chan)), w_large[4 * p * chan : (4 * p + 1) * chan])
        keep(wo, (p, slice(chan, 2 * chan)), w_large[(4 * p + 3) * chan : (4 * p + 4) * chan])

    def build(start, stop, col, num):
        area = pl.ds(col, num)

        def line(t, carry):
            b, a = lax.rem(t, 2), t // 2
            for hi, lo, shifts in ((eo_hi, eo_lo, (0, 1)), (oe_hi, oe_lo, (-1, 2))):
                for place_at, shift in zip((slice(0, chan), slice(chan, 2 * chan)), shifts):
                    values = lat[t, pl.ds(8 + 2 * col + shift, num, stride=2), :]
                    hi[b, a, area, place_at], lo[b, a, area, place_at] = split(values)
            return carry

        lax.fori_loop(start, stop, line, 0)

    def go(s, member):
        return pltpu.make_async_remote_copy(
            src_ref=emb.at[s, member], dst_ref=recv.at[s, me], send_sem=go_send.at[s, member],
            recv_sem=go_recv.at[s, me], device_id=place(member), device_id_type=MESH,
        )

    def arrival(s, member):
        return pltpu.make_async_remote_copy(
            src_ref=emb.at[s, member], dst_ref=recv.at[s, member], send_sem=go_send.at[s, member],
            recv_sem=go_recv.at[s, member], device_id=place(member), device_id_type=MESH,
        )

    def embed(s, part, row, row_num, col, col_num):
        def taps(hi, lo, p):
            where = (p % 2, pl.ds(row + p // 2, row_num), pl.ds(col, col_num))
            return tuple(ref[where].reshape(row_num * col_num, 2 * chan) for ref in (hi, lo))

        def pair(ref, index):
            return ref[0, index], ref[1, index]

        wide = dot3(taps(eo_hi, eo_lo, 1), pair(wc, 0)) + dot3(taps(eo_hi, eo_lo, 2), pair(wc, 1))
        thin = dot3(taps(eo_hi, eo_lo, 0), pair(we, 0)) + dot3(taps(eo_hi, eo_lo, 3), pair(we, 1))
        for p in range(4):
            thin = thin + dot3(taps(oe_hi, oe_lo, p), pair(wo, p))
        joined = jnp.concatenate([wide[:, :half], wide[:, half:] + thin], axis=-1)
        emb[s, pl.ds(part * (members // 4), members // 4)] = layer_norm(joined, gain_embed[...]).reshape(
            members // 4, lines, runs, groups, feat
        )

    def send_go(s, part):
        def send(step, carry):
            member = part * (members // 4) + lax.rem(me + step, members // 4)

            @pl.when(member != me)
            def _():
                go(s, member).start()

            return carry

        lax.fori_loop(0, members // 4, send, 0)

    pieces[0].wait()
    load(3).wait()
    def center(part):
        embed(0, part, strip * part, strip, quarter_cols, 2 * quarter_cols)

    build(strip_lines * first, strip_lines * first + strip_lines + 2, quarter_cols, 2 * quarter_cols)
    center(first)
    pieces[1].wait()
    pieces[2].wait()
    col_edge[0] = lat[pl.ds(1, rows), 8, :]
    col_edge[1] = lat[pl.ds(1, rows), cols + 7, :]
    number = lambda flag: jnp.where(flag, 1, 0)
    vertical = number(up) + number(down)
    horizontal = 1 + number(west) + number(east)
    pl.semaphore_wait(barrier, members - 1 + vertical * horizontal)

    both = jnp.logical_and
    left_pad, right_pad = pl.ds(0, 8), pl.ds(cols + 8, 8)
    head_cols, tail_cols = pl.ds(0, 8), pl.ds(cols - 8, 8)
    middle = pl.ds(8, cols)
    plan = [
        (west, east, (r, c - 1), col_edge.at[0], col_halo.at[1]),
        (east, west, (r, c + 1), col_edge.at[1], col_halo.at[0]),
        (up, down, (r - 1, c), latent.at[0], lat.at[rows + 1, middle]),
        (down, up, (r + 1, c), latent.at[rows - 1], lat.at[0, middle]),
        (both(up, west), both(down, east), (r - 1, c - 1), latent.at[0, head_cols], lat.at[rows + 1, right_pad]),
        (both(up, east), both(down, west), (r - 1, c + 1), latent.at[0, tail_cols], lat.at[rows + 1, left_pad]),
        (both(down, west), both(up, east), (r + 1, c - 1), latent.at[rows - 1, head_cols], lat.at[0, right_pad]),
        (both(down, east), both(up, west), (r + 1, c + 1), latent.at[rows - 1, tail_cols], lat.at[0, left_pad]),
    ]

    def halo_copy(index):
        _, _, target, source, destination = plan[index]
        return pltpu.make_async_remote_copy(
            src_ref=source, dst_ref=destination, send_sem=halo_send.at[index],
            recv_sem=halo_recv.at[index], device_id=target, device_id_type=MESH,
        )

    def send_halo(indices):
        for index in indices:
            @pl.when(plan[index][0])
            def _(index=index):
                halo_copy(index).start()

    send_halo(range(8))
    send_go(0, first)

    def await_halo(indices):
        for index in indices:
            _, arrives, _, _, destination = plan[index]

            @pl.when(arrives)
            def _(index=index):
                halo_copy(index).wait_recv()

            @pl.when(jnp.logical_not(arrives))
            def _(destination=destination):
                destination[...] = jnp.zeros(destination.shape, F32)

    pieces[3].wait()
    build(third_line, third_line + strip_lines, quarter_cols, 2 * quarter_cols)
    center(third)
    send_go(0, third)
    pieces[4].wait()
    pieces[5].wait()
    await_halo((2, 3))
    outer = 3 * strip_lines + 2
    build(outer * (1 - side), outer * (1 - side) + strip_lines, quarter_cols, 2 * quarter_cols)
    center(second)
    send_go(0, second)
    build(outer * side, outer * side + strip_lines, quarter_cols, 2 * quarter_cols)
    center(fourth)
    send_go(0, fourth)
    recv[0, me] = emb[0, me]

    await_halo((0, 1, 4, 5, 6, 7))
    pieces[6].wait()
    pieces[7].wait()

    def edge(t, carry):
        lat[t + 1, pl.ds(7, 1)] = col_halo[0, pl.ds(t, 1)]
        lat[t + 1, pl.ds(cols + 8, 1)] = col_halo[1, pl.ds(t, 1)]
        return carry

    lax.fori_loop(0, rows, edge, 0)

    def outside(step, carry):
        part = lax.rem(2 * (1 - side + step) + step // 2, 4)
        low = lax.rem(part, 2)
        col = pl.multiple_of(part // 2 * (3 * quarter_cols), quarter_cols)
        line = 4 * strip * low
        build(line, line + 4 * strip + 2, col, quarter_cols)
        embed(1, part, 2 * strip * low, 2 * strip, col, quarter_cols)
        send_go(1, part)
        return carry

    lax.fori_loop(0, 4, outside, 0)
    recv[1, me] = emb[1, me]

    for index in range(4, 11):
        load(index).wait()

    for ref, source in ((wq, w_qkv), (wp, w_proj), (wu, w_up), (wd, w_down)):
        ref[0], ref[1] = split(source[...])

    slot = lax.broadcasted_iota(jnp.int32, (nest, members), 0) // LANES
    number_of = lax.rem(slot, per) * col_count + slot // per
    spread = (number_of == lax.broadcasted_iota(jnp.int32, (nest, members), 1)).astype(F32)
    same = lax.rem(lax.broadcasted_iota(jnp.int32, (nest, nest), 0), LANES) == lax.rem(
        lax.broadcasted_iota(jnp.int32, (nest, nest), 1), LANES
    )
    exact = functools.partial(
        lax.dot_general, precision=lax.Precision.HIGHEST, preferred_element_type=F32
    )

    def widen(h, carry):
        tall = exact(spread, pos_bias[h], (((1,), (0,)), ((), ())))
        bias[h] = jnp.where(same, exact(tall, spread, (((1,), (1,)), ((), ()))), -1e30)
        return carry

    lax.fori_loop(0, HEADS, widen, 0)

    whole = PARTS == 1 or lines == 1
    splits = 1 if whole else lines

    def home(s, owner, part):
        start = owner * share
        if s == 0:
            place_at = out.at[start // (2 * quarter_cols * lines)]
            column = (quarter_cols + lax.rem(start, 2 * quarter_cols)) // groups
            return place_at.at[:, pl.ds(column, runs)] if whole else place_at.at[part, pl.ds(column, runs)]
        row = lax.rem(start, tile_rows * quarter_cols) // quarter_cols
        column = (start // (tile_rows * quarter_cols) * (3 * quarter_cols) + lax.rem(start, quarter_cols)) // groups
        if share <= quarter_cols:
            return out.at[row, :, pl.ds(column, runs)]
        if whole:
            return out.at[pl.ds(row // lines, runs), :, column]
        return out.at[row // lines + part, :, column]

    def ready(s, member, part):
        return done.at[s, member] if whole else done.at[s, member, part]

    def back(s, member, part):
        return pltpu.make_async_remote_copy(
            src_ref=ready(s, member, part), dst_ref=home(s, me, part), send_sem=back_send.at[s, part, member],
            recv_sem=back_recv.at[s, part, me], device_id=place(member), device_id_type=MESH,
        )

    def back_arrival(s, owner, part):
        return pltpu.make_async_remote_copy(
            src_ref=ready(s, owner, part), dst_ref=home(s, owner, part), send_sem=back_send.at[s, part, owner],
            recv_sem=back_recv.at[s, part, owner], device_id=place(owner), device_id_type=MESH,
        )

    def own(s, part):
        return pltpu.make_async_copy(ready(s, me, part), home(s, me, part), back_recv.at[s, part, me])

    lane_head = lax.broadcasted_iota(jnp.int32, (1, lane), 1) // head
    only = [jnp.where(lane_head == h, 1.0, 0.0).astype(BF16) for h in range(lane // head)]
    scale = 1.0 / (head**0.5)

    def block(s, b):
        where = (s, slice(None), b // runs, lax.rem(b, runs))
        rows_of = [where + (slice(first_group, first_group + LANES),) for first_group in range(0, groups, LANES)]
        x = jnp.concatenate([recv[rows_in].reshape(nest, feat) for rows_in in rows_of], axis=0)
        normed = split(layer_norm(x, gain_attn[...]))
        qkv = dot3(normed, (wq[0], wq[1]))
        q = split(qkv[:, :feat] * scale)
        k = split(qkv[:, feat : 2 * feat])
        v = split(qkv[:, 2 * feat :])
        pieces_of = []
        for start in range(0, tokens, nest):
            q_in, k_in, v_in = (tuple(part[start : start + nest] for part in pair) for pair in (q, k, v))
            tiles = []
            for tile in range(0, feat, lane):
                q_tile, k_tile, v_tile = (
                    tuple(part[:, tile : tile + lane] for part in pair) for pair in (q_in, k_in, v_in)
                )
                k_wide = jnp.concatenate([jnp.concatenate([part, part], axis=1) for part in k_tile], axis=0)
                v_line = jnp.concatenate(v_tile, axis=1)
                v_wide = jnp.concatenate([v_line, v_line], axis=0)
                mixed = jnp.zeros((nest, lane), F32)
                for h in range(0, lane // head, pack):
                    heads = range(h, h + pack)
                    q_tall = jnp.concatenate(
                        [jnp.concatenate([part * only[g] for part in q_tile], axis=1) for g in heads], axis=0
                    )
                    products = dot(q_tall, k_wide, ((1,), (1,)))
                    first_head = tile // head + h
                    scores = products[:, :nest] + products[:, nest:] + bias[
                        first_head : first_head + pack
                    ].reshape(pack * nest, nest)
                    expd = jnp.exp(scores - jnp.max(scores, axis=-1, keepdims=True))
                    probs = split(expd * (1.0 / jnp.sum(expd, axis=-1, keepdims=True)))
                    products = dot(jnp.concatenate(probs, axis=1), v_wide)
                    wide = products[:, :lane] + products[:, lane:]
                    for g in heads:
                        mixed = mixed + jnp.where(lane_head == g, wide[(g - h) * nest : (g - h + 1) * nest], 0.0)
                tiles.append(mixed)
            pieces_of.append(jnp.concatenate(tiles, axis=1))
        mixed = jnp.concatenate(pieces_of, axis=0)
        after = x + dot3(split(mixed), (wp[0], wp[1]))
        hidden = gelu(dot3(split(layer_norm(after, gain_mlp[...])), (wu[0], wu[1])))
        result = after + dot3(split(hidden), (wd[0], wd[1]))
        for index, rows_in in enumerate(rows_of):
            done[rows_in] = result[index * nest : (index + 1) * nest].reshape(members, LANES, feat)

    def process(s, carry):
        def await_one(step, inner):
            arrival(s, other(step)).wait_recv()
            return inner

        lax.fori_loop(0, members - 1, await_one, 0)

        def some(part, inner):
            def work(b, inside):
                block(s, b)
                return inside

            count = lines * runs // splits
            lax.fori_loop(part * count, part * count + count, work, 0)

            for stage in range(STAGES):
                @pl.when(s == stage)
                def _(stage=stage):
                    def send(step, inside):
                        back(stage, other(step), part).start()
                        return inside

                    lax.fori_loop(0, members - 1, send, 0)
                    own(stage, part).start()

            return inner

        lax.fori_loop(0, splits, some, 0)
        return carry

    lax.fori_loop(0, STAGES, process, 0)

    for s in range(STAGES):
        def sent(step, carry, s=s):
            member = other(step)
            go(s, member).wait_send()
            for part in range(splits):
                back(s, member, part).wait_send()
            return carry

        lax.fori_loop(0, members - 1, sent, 0)
    for index in range(8):
        @pl.when(plan[index][0])
        def _(index=index):
            halo_copy(index).wait_send()
    for s in range(STAGES):
        def landed(step, carry, s=s):
            for part in range(splits):
                back_arrival(s, other(step), part).wait_recv()
            return carry

        lax.fori_loop(0, members - 1, landed, 0)
        for part in range(splits):
            own(s, part).wait()


def per_device(
    latent, w_small, w_large, gain_embed, gain_attn, w_qkv, pos_bias, w_proj, gain_mlp, w_up, w_down
):
    row_count = lax.axis_size("rows")
    col_count = lax.axis_size("cols")
    samples, rows, cols, chan = latent.shape
    tile_rows, tile_cols = rows // 2, cols // 2
    feat = gain_embed.shape[0]
    half = feat // 2
    members = pos_bias.shape[1]
    phases = row_count // (members // col_count)
    share = tile_rows * tile_cols // STAGES // members
    groups = max(8, min(share, 256 // members))
    pixels = pltpu.VMEM((2, tile_rows + 1, tile_cols, 2 * chan), BF16)
    lines = max(1, share // (tile_cols // 2))
    exchange = pltpu.VMEM((STAGES, members, lines, share // groups // lines, groups, feat), F32)
    dma = pltpu.SemaphoreType.DMA
    inputs = (
        latent[0], w_small, w_large, gain_embed[None], gain_attn[None], w_qkv, pos_bias, w_proj,
        gain_mlp[None], w_up, w_down,
    )
    halves = lambda *shape: pltpu.VMEM((2,) + shape, BF16)
    out_bytes = tile_rows * tile_cols * feat * 4
    out = pl.pallas_call(
        functools.partial(block_kernel, (row_count, col_count, members, phases, groups)),
        name="crossformer_block",
        out_shape=pltpu.VMEM((tile_rows // lines, lines, tile_cols // groups, groups, feat), F32),
        in_specs=[pl.BlockSpec(memory_space=pltpu.HBM)] * 11,
        out_specs=pl.BlockSpec(memory_space=pltpu.VMEM),
        scratch_shapes=[pltpu.VMEM((rows + 2, cols + 16, chan), F32)]
        + [pltpu.VMEM(array.shape, F32) for array in inputs[1:]]
        + [
            pixels, pixels, pixels, pixels,
            halves(2, 2 * chan, feat),
            halves(2, 2 * chan, half),
            halves(4, 2 * chan, half),
            halves(*w_qkv.shape),
            halves(*w_proj.shape),
            halves(*w_up.shape),
            halves(*w_down.shape),
            pltpu.VMEM((HEADS, members * LANES, members * LANES), F32),
            exchange, exchange, exchange,
            pltpu.VMEM((2, rows, chan), F32),
            pltpu.VMEM((2, rows, chan), F32),
            dma((8,)), dma((8,)),
            dma((STAGES, members)), dma((STAGES, members)),
            dma((STAGES, lines, members)), dma((STAGES, lines, members)),
            dma((11,)), dma((8,)),
        ],
        compiler_params=pltpu.CompilerParams(
            collective_id=0, has_side_effects=True, vmem_limit_bytes=67043328 - out_bytes
        ),
    )(*inputs)
    return out.reshape(samples, tile_rows, tile_cols, feat)


def solution(mesh):
    in_specs = (P(None, "rows", "cols", None),) + (P(),) * 10
    out_specs = P(None, "rows", "cols", None)
    return jax.shard_map(
        per_device, mesh=mesh, in_specs=in_specs, out_specs=out_specs, check_vma=False
    )
```

```python
import functools

import jax
import jax.numpy as jnp
from jax import lax
from jax.experimental import pallas as pl
from jax.experimental.pallas import tpu as pltpu
from jax.sharding import PartitionSpec as P

HEADS = 8
STAGES = 2
PARTS = 2
LANES = 8
MESH = pl.DeviceIdType.MESH
F32 = jnp.float32
BF16 = jnp.bfloat16


def split(values):
    high = values.astype(BF16)
    return high, (values - high.astype(F32)).astype(BF16)


def dot(left, right, dims=((1,), (0,))):
    return lax.dot_general(left, right, (dims, ((), ())), preferred_element_type=F32)


def dot3(left, right, dims=((1,), (0,))):
    left_hi, left_lo = left
    right_hi, right_lo = right
    return (
        dot(left_hi, right_lo, dims) + dot(left_lo, right_hi, dims) + dot(left_hi, right_hi, dims)
    )


def layer_norm(values, gain):
    center = values - jnp.mean(values, axis=-1, keepdims=True)
    spread = jnp.mean(center * center, axis=-1, keepdims=True)
    return center * lax.rsqrt(spread + 1e-05) * gain


def gelu(values):
    return 0.5 * values * (1.0 + lax.erf(values * 0.7071067811865476))


def block_kernel(
    sizes,
    *refs,
):
    inputs, out = refs[:11], refs[11]
    latent = inputs[0]
    (
        lat, w_small, w_large, gain_embed, gain_attn, w_qkv, pos_bias, w_proj, gain_mlp, w_up, w_down,
        eo_hi, eo_lo, oe_hi, oe_lo, wc, we, wo, wq, wp, wu, wd, bias,
        emb, recv, done, col_halo, col_edge,
        halo_send, halo_recv, go_send, go_recv, back_send, back_recv, load_sem, part_sem, side_sem,
    ) = refs[12:]
    loaded = (
        None, w_small, w_large, gain_embed, gain_attn, w_qkv, pos_bias, w_proj, gain_mlp, w_up, w_down,
    )
    row_count, col_count, members, phases, groups = sizes
    rows, cols, chan = latent.shape
    tile_rows, tile_cols = rows // 2, cols // 2
    feat = gain_embed.shape[1]
    half = feat // 2
    quarter_cols = tile_cols // 4
    share = tile_rows * tile_cols // STAGES // members
    lines = max(1, share // (2 * quarter_cols))
    runs = share // groups // lines
    tokens = members * groups
    head = feat // HEADS
    nest = members * LANES
    lane = min(feat, 128)
    pack = min(lane // head, max(1, 1024 // nest))
    half_members = members // 2
    half_cols = col_count // 2
    per = members // col_count
    strip = tile_rows // 4

    r = lax.axis_index("rows")
    c = lax.axis_index("cols")
    core = lax.rem(r, phases)
    side, spot = c // half_cols, lax.rem(c, half_cols)
    band = r // phases
    me = side * half_members + spot * per + band

    def place(member):
        return (
            lax.rem(member, per) * phases + core,
            member // half_members * half_cols + lax.rem(member, half_members) // per,
        )

    def other(step):
        group = step // per
        shift = col_count // 2 + (group + 1) // 2 * (2 * lax.rem(group, 2) - 1)
        to_col = lax.rem(c + shift + col_count, col_count)
        return to_col * per + lax.rem(band + step + 1, per)

    first, fourth = 2 - side, 3 * side
    second, third = 3 - fourth, 3 - first
    left_col, right_col = 2 * quarter_cols - 8, 6 * quarter_cols + 8
    wide = right_col - left_col
    strip_lines = 2 * strip
    third_line = strip_lines * third + 2 * side

    def piece(index, row, row_num, col, col_num):
        return pltpu.make_async_copy(
            latent.at[pl.ds(row, row_num), pl.ds(col, col_num)],
            lat.at[pl.ds(row + 1, row_num), pl.ds(col + 8, col_num)],
            part_sem.at[index],
        )

    pieces = [
        piece(0, strip_lines * first - 1, strip_lines + 2, left_col, wide),
        piece(1, 0, rows, 0, 8),
        piece(2, 0, rows, cols - 8, 8),
        piece(3, third_line - 1, strip_lines, left_col, wide),
        piece(4, 0, strip_lines - 1, left_col, wide),
        piece(5, 3 * strip_lines + 1, strip_lines - 1, left_col, wide),
        piece(6, 0, rows, 8, left_col - 8),
        piece(7, 0, rows, right_col, cols - 8 - right_col),
    ]

    def load(index):
        return pltpu.make_async_copy(inputs[index], loaded[index], load_sem.at[index])

    pieces[0].start()
    load(1).start()
    load(2).start()
    load(3).start()

    barrier = pltpu.get_barrier_semaphore()

    def greet(step, carry):
        opposite = (1 - side) * half_members + lax.rem(me + step, half_members)
        pl.semaphore_signal(barrier, inc=1, device_id=place(opposite), device_id_type=MESH)
        return carry

    lax.fori_loop(0, half_members, greet, 0)
    up, down = r > 0, r < row_count - 1
    west, east = c > 0, c < col_count - 1
    near_west = jnp.logical_and(west, c != half_cols)
    near_east = jnp.logical_and(east, c != half_cols - 1)
    for ok, dc in ((near_west, -1), (near_east, 1)):
        @pl.when(ok)
        def _(dc=dc):
            pl.semaphore_signal(barrier, inc=1, device_id=(r, c + dc), device_id_type=MESH)

    for row_ok, dr in ((up, -1), (down, 1)):
        for col_ok, dc in ((True, 0), (west, -1), (east, 1)):
            ok = row_ok if col_ok is True else jnp.logical_and(row_ok, col_ok)

            @pl.when(ok)
            def _(dr=dr, dc=dc):
                pl.semaphore_signal(barrier, inc=1, device_id=(r + dr, c + dc), device_id_type=MESH)

    for index in range(1, 8):
        pieces[index].start()
    for index in range(4, 11):
        load(index).start()

    def keep(ref, index, values):
        ref[(0,) + index], ref[(1,) + index] = split(values)

    load(1).wait()
    load(2).wait()
    for p in range(2):
        keep(wc, (p, slice(None), slice(0, half)), w_small[2 * p * chan : 2 * (p + 1) * chan])
        start = (p + 1) * 4 * chan + chan
        keep(wc, (p, slice(None), slice(half, feat)), w_large[start : start + 2 * chan])
        start = 3 * p * 4 * chan + chan
        keep(we, (p,), w_large[start : start + 2 * chan])
    for p in range(4):
        keep(wo, (p, slice(0, chan)), w_large[4 * p * chan : (4 * p + 1) * chan])
        keep(wo, (p, slice(chan, 2 * chan)), w_large[(4 * p + 3) * chan : (4 * p + 4) * chan])

    def build(start, stop, col, num):
        area = pl.ds(col, num)

        def line(t, carry):
            b, a = lax.rem(t, 2), t // 2
            for hi, lo, shifts in ((eo_hi, eo_lo, (0, 1)), (oe_hi, oe_lo, (-1, 2))):
                for place_at, shift in zip((slice(0, chan), slice(chan, 2 * chan)), shifts):
                    values = lat[t, pl.ds(8 + 2 * col + shift, num, stride=2), :]
                    hi[b, a, area, place_at], lo[b, a, area, place_at] = split(values)
            return carry

        lax.fori_loop(start, stop, line, 0)

    def go(s, member):
        return pltpu.make_async_remote_copy(
            src_ref=emb.at[s, member], dst_ref=recv.at[s, me], send_sem=go_send.at[s, member],
            recv_sem=go_recv.at[s, me], device_id=place(member), device_id_type=MESH,
        )

    def arrival(s, member):
        return pltpu.make_async_remote_copy(
            src_ref=emb.at[s, member], dst_ref=recv.at[s, member], send_sem=go_send.at[s, member],
            recv_sem=go_recv.at[s, member], device_id=place(member), device_id_type=MESH,
        )

    def embed(s, part, row, row_num, col, col_num):
        def taps(hi, lo, p):
            where = (p % 2, pl.ds(row + p // 2, row_num), pl.ds(col, col_num))
            return tuple(ref[where].reshape(row_num * col_num, 2 * chan) for ref in (hi, lo))

        def pair(ref, index):
            return ref[0, index], ref[1, index]

        wide = dot3(taps(eo_hi, eo_lo, 1), pair(wc, 0)) + dot3(taps(eo_hi, eo_lo, 2), pair(wc, 1))
        thin = dot3(taps(eo_hi, eo_lo, 0), pair(we, 0)) + dot3(taps(eo_hi, eo_lo, 3), pair(we, 1))
        for p in range(4):
            thin = thin + dot3(taps(oe_hi, oe_lo, p), pair(wo, p))
        joined = jnp.concatenate([wide[:, :half], wide[:, half:] + thin], axis=-1)
        emb[s, pl.ds(part * (members // 4), members // 4)] = layer_norm(joined, gain_embed[...]).reshape(
            members // 4, lines, runs, groups, feat
        )

    def send_go(s, part):
        def send(step, carry):
            member = part * (members // 4) + lax.rem(me + step, members // 4)

            @pl.when(member != me)
            def _():
                go(s, member).start()

            return carry

        lax.fori_loop(0, members // 4, send, 0)

    pieces[0].wait()
    load(3).wait()
    def center(part):
        embed(0, part, strip * part, strip, quarter_cols, 2 * quarter_cols)

    build(strip_lines * first, strip_lines * first + strip_lines + 2, quarter_cols, 2 * quarter_cols)
    center(first)
    pieces[1].wait()
    pieces[2].wait()
    col_edge[0] = lat[pl.ds(1, rows), 8, :]
    col_edge[1] = lat[pl.ds(1, rows), cols + 7, :]
    number = lambda flag: jnp.where(flag, 1, 0)
    vertical = number(up) + number(down)
    horizontal = 1 + number(west) + number(east)
    beside = number(near_west) + number(near_east)
    pl.semaphore_wait(barrier, half_members + vertical * horizontal + beside)
    mirror = (1 - side) * half_members + lax.rem(me, half_members)
    pl.semaphore_signal(side_sem, inc=1, device_id=place(mirror), device_id_type=MESH)

    both = jnp.logical_and
    left_pad, right_pad = pl.ds(0, 8), pl.ds(cols + 8, 8)
    head_cols, tail_cols = pl.ds(0, 8), pl.ds(cols - 8, 8)
    middle = pl.ds(8, cols)
    plan = [
        (west, east, (r, c - 1), col_edge.at[0], col_halo.at[1]),
        (east, west, (r, c + 1), col_edge.at[1], col_halo.at[0]),
        (up, down, (r - 1, c), latent.at[0], lat.at[rows + 1, middle]),
        (down, up, (r + 1, c), latent.at[rows - 1], lat.at[0, middle]),
        (both(up, west), both(down, east), (r - 1, c - 1), latent.at[0, head_cols], lat.at[rows + 1, right_pad]),
        (both(up, east), both(down, west), (r - 1, c + 1), latent.at[0, tail_cols], lat.at[rows + 1, left_pad]),
        (both(down, west), both(up, east), (r + 1, c - 1), latent.at[rows - 1, head_cols], lat.at[0, right_pad]),
        (both(down, east), both(up, west), (r + 1, c + 1), latent.at[rows - 1, tail_cols], lat.at[0, left_pad]),
    ]

    def halo_copy(index):
        _, _, target, source, destination = plan[index]
        return pltpu.make_async_remote_copy(
            src_ref=source, dst_ref=destination, send_sem=halo_send.at[index],
            recv_sem=halo_recv.at[index], device_id=target, device_id_type=MESH,
        )

    def send_halo(indices):
        for index in indices:
            @pl.when(plan[index][0])
            def _(index=index):
                halo_copy(index).start()

    send_halo(range(8))
    send_go(0, first)

    def await_halo(indices):
        for index in indices:
            _, arrives, _, _, destination = plan[index]

            @pl.when(arrives)
            def _(index=index):
                halo_copy(index).wait_recv()

            @pl.when(jnp.logical_not(arrives))
            def _(destination=destination):
                destination[...] = jnp.zeros(destination.shape, F32)

    pieces[3].wait()
    build(third_line, third_line + strip_lines, quarter_cols, 2 * quarter_cols)
    center(third)
    pl.semaphore_wait(side_sem, 1)
    send_go(0, third)
    pieces[4].wait()
    pieces[5].wait()
    await_halo((2, 3))
    outer = 3 * strip_lines + 2
    build(outer * (1 - side), outer * (1 - side) + strip_lines, quarter_cols, 2 * quarter_cols)
    center(second)
    send_go(0, second)
    build(outer * side, outer * side + strip_lines, quarter_cols, 2 * quarter_cols)
    center(fourth)
    send_go(0, fourth)
    recv[0, me] = emb[0, me]

    await_halo((0, 1, 4, 5, 6, 7))
    pieces[6].wait()
    pieces[7].wait()

    def edge(t, carry):
        lat[t + 1, pl.ds(7, 1)] = col_halo[0, pl.ds(t, 1)]
        lat[t + 1, pl.ds(cols + 8, 1)] = col_halo[1, pl.ds(t, 1)]
        return carry

    lax.fori_loop(0, rows, edge, 0)

    def outside(step, carry):
        part = lax.rem(2 * (1 - side + step) + step // 2, 4)
        low = lax.rem(part, 2)
        col = pl.multiple_of(part // 2 * (3 * quarter_cols), quarter_cols)
        line = 4 * strip * low
        build(line, line + 4 * strip + 2, col, quarter_cols)
        embed(1, part, 2 * strip * low, 2 * strip, col, quarter_cols)
        send_go(1, part)
        return carry

    lax.fori_loop(0, 4, outside, 0)
    recv[1, me] = emb[1, me]

    for index in range(4, 11):
        load(index).wait()

    for ref, source in ((wq, w_qkv), (wp, w_proj), (wu, w_up), (wd, w_down)):
        ref[0], ref[1] = split(source[...])

    slot = lax.broadcasted_iota(jnp.int32, (nest, members), 0) // LANES
    number_of = lax.rem(slot, per) * col_count + slot // per
    spread = (number_of == lax.broadcasted_iota(jnp.int32, (nest, members), 1)).astype(F32)
    same = lax.rem(lax.broadcasted_iota(jnp.int32, (nest, nest), 0), LANES) == lax.rem(
        lax.broadcasted_iota(jnp.int32, (nest, nest), 1), LANES
    )
    exact = functools.partial(
        lax.dot_general, precision=lax.Precision.HIGHEST, preferred_element_type=F32
    )

    def widen(h, carry):
        tall = exact(spread, pos_bias[h], (((1,), (0,)), ((), ())))
        bias[h] = jnp.where(same, exact(tall, spread, (((1,), (1,)), ((), ()))), -1e30)
        return carry

    lax.fori_loop(0, HEADS, widen, 0)

    whole = PARTS == 1 or lines == 1
    splits = 1 if whole else lines

    def home(s, owner, part):
        start = owner * share
        if s == 0:
            place_at = out.at[start // (2 * quarter_cols * lines)]
            column = (quarter_cols + lax.rem(start, 2 * quarter_cols)) // groups
            return place_at.at[:, pl.ds(column, runs)] if whole else place_at.at[part, pl.ds(column, runs)]
        row = lax.rem(start, tile_rows * quarter_cols) // quarter_cols
        column = (start // (tile_rows * quarter_cols) * (3 * quarter_cols) + lax.rem(start, quarter_cols)) // groups
        if share <= quarter_cols:
            return out.at[row, :, pl.ds(column, runs)]
        if whole:
            return out.at[pl.ds(row // lines, runs), :, column]
        return out.at[row // lines + part, :, column]

    def ready(s, member, part):
        return done.at[s, member] if whole else done.at[s, member, part]

    def back(s, member, part):
        return pltpu.make_async_remote_copy(
            src_ref=ready(s, member, part), dst_ref=home(s, me, part), send_sem=back_send.at[s, part, member],
            recv_sem=back_recv.at[s, part, me], device_id=place(member), device_id_type=MESH,
        )

    def back_arrival(s, owner, part):
        return pltpu.make_async_remote_copy(
            src_ref=ready(s, owner, part), dst_ref=home(s, owner, part), send_sem=back_send.at[s, part, owner],
            recv_sem=back_recv.at[s, part, owner], device_id=place(owner), device_id_type=MESH,
        )

    def own(s, part):
        return pltpu.make_async_copy(ready(s, me, part), home(s, me, part), back_recv.at[s, part, me])

    lane_head = lax.broadcasted_iota(jnp.int32, (1, lane), 1) // head
    only = [jnp.where(lane_head == h, 1.0, 0.0).astype(BF16) for h in range(lane // head)]
    scale = 1.0 / (head**0.5)

    def block(s, b):
        where = (s, slice(None), b // runs, lax.rem(b, runs))
        rows_of = [where + (slice(first_group, first_group + LANES),) for first_group in range(0, groups, LANES)]
        x = jnp.concatenate([recv[rows_in].reshape(nest, feat) for rows_in in rows_of], axis=0)
        normed = split(layer_norm(x, gain_attn[...]))
        qkv = dot3(normed, (wq[0], wq[1]))
        q = split(qkv[:, :feat] * scale)
        k = split(qkv[:, feat : 2 * feat])
        v = split(qkv[:, 2 * feat :])
        pieces_of = []
        for start in range(0, tokens, nest):
            q_in, k_in, v_in = (tuple(part[start : start + nest] for part in pair) for pair in (q, k, v))
            tiles = []
            for tile in range(0, feat, lane):
                q_tile, k_tile, v_tile = (
                    tuple(part[:, tile : tile + lane] for part in pair) for pair in (q_in, k_in, v_in)
                )
                k_wide = jnp.concatenate([jnp.concatenate([part, part], axis=1) for part in k_tile], axis=0)
                v_line = jnp.concatenate(v_tile, axis=1)
                v_wide = jnp.concatenate([v_line, v_line], axis=0)
                mixed = jnp.zeros((nest, lane), F32)
                for h in range(0, lane // head, pack):
                    heads = range(h, h + pack)
                    q_tall = jnp.concatenate(
                        [jnp.concatenate([part * only[g] for part in q_tile], axis=1) for g in heads], axis=0
                    )
                    products = dot(q_tall, k_wide, ((1,), (1,)))
                    first_head = tile // head + h
                    scores = products[:, :nest] + products[:, nest:] + bias[
                        first_head : first_head + pack
                    ].reshape(pack * nest, nest)
                    expd = jnp.exp(scores - jnp.max(scores, axis=-1, keepdims=True))
                    probs = split(expd * (1.0 / jnp.sum(expd, axis=-1, keepdims=True)))
                    products = dot(jnp.concatenate(probs, axis=1), v_wide)
                    wide = products[:, :lane] + products[:, lane:]
                    for g in heads:
                        mixed = mixed + jnp.where(lane_head == g, wide[(g - h) * nest : (g - h + 1) * nest], 0.0)
                tiles.append(mixed)
            pieces_of.append(jnp.concatenate(tiles, axis=1))
        mixed = jnp.concatenate(pieces_of, axis=0)
        after = x + dot3(split(mixed), (wp[0], wp[1]))
        hidden = gelu(dot3(split(layer_norm(after, gain_mlp[...])), (wu[0], wu[1])))
        result = after + dot3(split(hidden), (wd[0], wd[1]))
        for index, rows_in in enumerate(rows_of):
            done[rows_in] = result[index * nest : (index + 1) * nest].reshape(members, LANES, feat)

    def process(s, carry):
        def await_one(step, inner):
            arrival(s, other(step)).wait_recv()
            return inner

        lax.fori_loop(0, members - 1, await_one, 0)

        def some(part, inner):
            def work(b, inside):
                block(s, b)
                return inside

            count = lines * runs // splits
            lax.fori_loop(part * count, part * count + count, work, 0)

            for stage in range(STAGES):
                @pl.when(s == stage)
                def _(stage=stage):
                    def send(step, inside):
                        back(stage, other(step), part).start()
                        return inside

                    lax.fori_loop(0, members - 1, send, 0)
                    own(stage, part).start()

            return inner

        lax.fori_loop(0, splits, some, 0)
        return carry

    lax.fori_loop(0, STAGES, process, 0)

    for s in range(STAGES):
        def sent(step, carry, s=s):
            member = other(step)
            go(s, member).wait_send()
            for part in range(splits):
                back(s, member, part).wait_send()
            return carry

        lax.fori_loop(0, members - 1, sent, 0)
    for index in range(8):
        @pl.when(plan[index][0])
        def _(index=index):
            halo_copy(index).wait_send()
    for s in range(STAGES):
        def landed(step, carry, s=s):
            for part in range(splits):
                back_arrival(s, other(step), part).wait_recv()
            return carry

        lax.fori_loop(0, members - 1, landed, 0)
        for part in range(splits):
            own(s, part).wait()


def per_device(
    latent, w_small, w_large, gain_embed, gain_attn, w_qkv, pos_bias, w_proj, gain_mlp, w_up, w_down
):
    row_count = lax.axis_size("rows")
    col_count = lax.axis_size("cols")
    samples, rows, cols, chan = latent.shape
    tile_rows, tile_cols = rows // 2, cols // 2
    feat = gain_embed.shape[0]
    half = feat // 2
    members = pos_bias.shape[1]
    phases = row_count // (members // col_count)
    share = tile_rows * tile_cols // STAGES // members
    groups = max(8, min(share, 256 // members))
    pixels = pltpu.VMEM((2, tile_rows + 1, tile_cols, 2 * chan), BF16)
    lines = max(1, share // (tile_cols // 2))
    exchange = pltpu.VMEM((STAGES, members, lines, share // groups // lines, groups, feat), F32)
    dma = pltpu.SemaphoreType.DMA
    inputs = (
        latent[0], w_small, w_large, gain_embed[None], gain_attn[None], w_qkv, pos_bias, w_proj,
        gain_mlp[None], w_up, w_down,
    )
    halves = lambda *shape: pltpu.VMEM((2,) + shape, BF16)
    out_bytes = tile_rows * tile_cols * feat * 4
    out = pl.pallas_call(
        functools.partial(block_kernel, (row_count, col_count, members, phases, groups)),
        name="crossformer_block",
        out_shape=pltpu.VMEM((tile_rows // lines, lines, tile_cols // groups, groups, feat), F32),
        in_specs=[pl.BlockSpec(memory_space=pltpu.HBM)] * 11,
        out_specs=pl.BlockSpec(memory_space=pltpu.VMEM),
        scratch_shapes=[pltpu.VMEM((rows + 2, cols + 16, chan), F32)]
        + [pltpu.VMEM(array.shape, F32) for array in inputs[1:]]
        + [
            pixels, pixels, pixels, pixels,
            halves(2, 2 * chan, feat),
            halves(2, 2 * chan, half),
            halves(4, 2 * chan, half),
            halves(*w_qkv.shape),
            halves(*w_proj.shape),
            halves(*w_up.shape),
            halves(*w_down.shape),
            pltpu.VMEM((HEADS, members * LANES, members * LANES), F32),
            exchange, exchange, exchange,
            pltpu.VMEM((2, rows, chan), F32),
            pltpu.VMEM((2, rows, chan), F32),
            dma((8,)), dma((8,)),
            dma((STAGES, members)), dma((STAGES, members)),
            dma((STAGES, lines, members)), dma((STAGES, lines, members)),
            dma((11,)), dma((8,)),
            pltpu.SemaphoreType.REGULAR,
        ],
        compiler_params=pltpu.CompilerParams(
            collective_id=0, has_side_effects=True, vmem_limit_bytes=67043328 - out_bytes
        ),
    )(*inputs)
    return out.reshape(samples, tile_rows, tile_cols, feat)


def solution(mesh):
    in_specs = (P(None, "rows", "cols", None),) + (P(),) * 10
    out_specs = P(None, "rows", "cols", None)
    return jax.shard_map(
        per_device, mesh=mesh, in_specs=in_specs, out_specs=out_specs, check_vma=False
    )
```

```python
import functools

import jax
import jax.numpy as jnp
from jax import lax
from jax.experimental import pallas as pl
from jax.experimental.pallas import tpu as pltpu
from jax.sharding import PartitionSpec as P

HEADS = 8
STAGES = 2
PARTS = 2
LANES = 8
MESH = pl.DeviceIdType.MESH
F32 = jnp.float32
BF16 = jnp.bfloat16


def split(values):
    high = values.astype(BF16)
    return high, (values - high.astype(F32)).astype(BF16)


def dot(left, right, dims=((1,), (0,))):
    return lax.dot_general(left, right, (dims, ((), ())), preferred_element_type=F32)


def dot3(left, right, dims=((1,), (0,))):
    left_hi, left_lo = left
    right_hi, right_lo = right
    return (
        dot(left_hi, right_lo, dims) + dot(left_lo, right_hi, dims) + dot(left_hi, right_hi, dims)
    )


def layer_norm(values, gain):
    center = values - jnp.mean(values, axis=-1, keepdims=True)
    spread = jnp.mean(center * center, axis=-1, keepdims=True)
    return center * lax.rsqrt(spread + 1e-05) * gain


def gelu(values):
    return 0.5 * values * (1.0 + lax.erf(values * 0.7071067811865476))


def block_kernel(
    sizes,
    *refs,
):
    inputs, out = refs[:11], refs[11]
    latent = inputs[0]
    (
        lat, w_small, w_large, gain_embed, gain_attn, w_qkv, pos_bias, w_proj, gain_mlp, w_up, w_down,
        eo_hi, eo_lo, oe_hi, oe_lo, wc, we, wo, wq, wp, wu, wd, bias,
        emb, recv, done, col_halo, col_edge,
        halo_send, halo_recv, go_send, go_recv, back_send, back_recv, load_sem, part_sem, side_sem,
    ) = refs[12:]
    loaded = (
        None, w_small, w_large, gain_embed, gain_attn, w_qkv, pos_bias, w_proj, gain_mlp, w_up, w_down,
    )
    row_count, col_count, members, phases, groups = sizes
    rows, cols, chan = latent.shape
    tile_rows, tile_cols = rows // 2, cols // 2
    feat = gain_embed.shape[1]
    half = feat // 2
    quarter_cols = tile_cols // 4
    share = tile_rows * tile_cols // STAGES // members
    lines = max(1, share // (2 * quarter_cols))
    runs = share // groups // lines
    tokens = members * groups
    head = feat // HEADS
    nest = members * LANES
    lane = min(feat, 128)
    pack = min(lane // head, max(1, 1024 // nest))
    half_members = members // 2
    half_cols = col_count // 2
    per = members // col_count
    strip = tile_rows // 4

    r = lax.axis_index("rows")
    c = lax.axis_index("cols")
    core = lax.rem(r, phases)
    side, spot = c // half_cols, lax.rem(c, half_cols)
    band = r // phases
    me = side * half_members + spot * per + band

    def place(member):
        return (
            lax.rem(member, per) * phases + core,
            member // half_members * half_cols + lax.rem(member, half_members) // per,
        )

    def other(step):
        group = step // per
        shift = col_count // 2 + (group + 1) // 2 * (2 * lax.rem(group, 2) - 1)
        to_col = lax.rem(c + shift + col_count, col_count)
        return to_col * per + lax.rem(band + step + 1, per)

    first, fourth = 2 - side, 3 * side
    second, third = 3 - fourth, 3 - first
    left_col, right_col = 2 * quarter_cols - 8, 6 * quarter_cols + 8
    wide = right_col - left_col
    strip_lines = 2 * strip
    third_line = strip_lines * third + 2 * side

    def piece(index, row, row_num, col, col_num):
        return pltpu.make_async_copy(
            latent.at[pl.ds(row, row_num), pl.ds(col, col_num)],
            lat.at[pl.ds(row + 1, row_num), pl.ds(col + 8, col_num)],
            part_sem.at[index],
        )

    pieces = [
        piece(0, strip_lines * first - 1, strip_lines + 2, left_col, wide),
        piece(1, 0, rows, 0, 8),
        piece(2, 0, rows, cols - 8, 8),
        piece(3, third_line - 1, strip_lines, left_col, wide),
        piece(4, 0, strip_lines - 1, left_col, wide),
        piece(5, 3 * strip_lines + 1, strip_lines - 1, left_col, wide),
        piece(6, 0, rows, 8, left_col - 8),
        piece(7, 0, rows, right_col, cols - 8 - right_col),
    ]

    def load(index):
        return pltpu.make_async_copy(inputs[index], loaded[index], load_sem.at[index])

    pieces[0].start()
    load(1).start()
    load(2).start()
    load(3).start()

    barrier = pltpu.get_barrier_semaphore()

    def greet(step, carry):
        opposite = (1 - side) * half_members + lax.rem(me + step, half_members)
        pl.semaphore_signal(barrier, inc=1, device_id=place(opposite), device_id_type=MESH)
        return carry

    lax.fori_loop(0, half_members, greet, 0)
    up, down = r > 0, r < row_count - 1
    west, east = c > 0, c < col_count - 1
    near_west = jnp.logical_and(west, c != half_cols)
    near_east = jnp.logical_and(east, c != half_cols - 1)
    for ok, dc in ((near_west, -1), (near_east, 1)):
        @pl.when(ok)
        def _(dc=dc):
            pl.semaphore_signal(barrier, inc=1, device_id=(r, c + dc), device_id_type=MESH)

    for row_ok, dr in ((up, -1), (down, 1)):
        for col_ok, dc in ((True, 0), (west, -1), (east, 1)):
            ok = row_ok if col_ok is True else jnp.logical_and(row_ok, col_ok)

            @pl.when(ok)
            def _(dr=dr, dc=dc):
                pl.semaphore_signal(barrier, inc=1, device_id=(r + dr, c + dc), device_id_type=MESH)

    for index in range(1, 8):
        pieces[index].start()
    for index in range(4, 11):
        load(index).start()

    def keep(ref, index, values):
        ref[(0,) + index], ref[(1,) + index] = split(values)

    load(1).wait()
    load(2).wait()
    for p in range(2):
        keep(wc, (p, slice(None), slice(0, half)), w_small[2 * p * chan : 2 * (p + 1) * chan])
        start = (p + 1) * 4 * chan + chan
        keep(wc, (p, slice(None), slice(half, feat)), w_large[start : start + 2 * chan])
        start = 3 * p * 4 * chan + chan
        keep(we, (p,), w_large[start : start + 2 * chan])
    for p in range(4):
        keep(wo, (p, slice(0, chan)), w_large[4 * p * chan : (4 * p + 1) * chan])
        keep(wo, (p, slice(chan, 2 * chan)), w_large[(4 * p + 3) * chan : (4 * p + 4) * chan])

    def build(start, stop, col, num):
        area = pl.ds(col, num)

        def line(t, carry):
            b, a = lax.rem(t, 2), t // 2
            for hi, lo, shifts in ((eo_hi, eo_lo, (0, 1)), (oe_hi, oe_lo, (-1, 2))):
                for place_at, shift in zip((slice(0, chan), slice(chan, 2 * chan)), shifts):
                    values = lat[t, pl.ds(8 + 2 * col + shift, num, stride=2), :]
                    hi[b, a, area, place_at], lo[b, a, area, place_at] = split(values)
            return carry

        lax.fori_loop(start, stop, line, 0)

    def go(s, member):
        return pltpu.make_async_remote_copy(
            src_ref=emb.at[s, member], dst_ref=recv.at[s, me], send_sem=go_send.at[s, member],
            recv_sem=go_recv.at[s, me], device_id=place(member), device_id_type=MESH,
        )

    def arrival(s, member):
        return pltpu.make_async_remote_copy(
            src_ref=emb.at[s, member], dst_ref=recv.at[s, member], send_sem=go_send.at[s, member],
            recv_sem=go_recv.at[s, member], device_id=place(member), device_id_type=MESH,
        )

    def embed(s, part, row, row_num, col, col_num):
        def taps(hi, lo, p):
            where = (p % 2, pl.ds(row + p // 2, row_num), pl.ds(col, col_num))
            return tuple(ref[where].reshape(row_num * col_num, 2 * chan) for ref in (hi, lo))

        def pair(ref, index):
            return ref[0, index], ref[1, index]

        wide = dot3(taps(eo_hi, eo_lo, 1), pair(wc, 0)) + dot3(taps(eo_hi, eo_lo, 2), pair(wc, 1))
        thin = dot3(taps(eo_hi, eo_lo, 0), pair(we, 0)) + dot3(taps(eo_hi, eo_lo, 3), pair(we, 1))
        for p in range(4):
            thin = thin + dot3(taps(oe_hi, oe_lo, p), pair(wo, p))
        joined = jnp.concatenate([wide[:, :half], wide[:, half:] + thin], axis=-1)
        emb[s, pl.ds(part * (members // 4), members // 4)] = layer_norm(joined, gain_embed[...]).reshape(
            members // 4, lines, runs, groups, feat
        )

    def send_go(s, part):
        def send(step, carry):
            member = part * (members // 4) + lax.rem(me + step, members // 4)

            @pl.when(member != me)
            def _():
                go(s, member).start()

            return carry

        lax.fori_loop(0, members // 4, send, 0)

    pieces[0].wait()
    load(3).wait()
    def center(part):
        embed(0, part, strip * part, strip, quarter_cols, 2 * quarter_cols)

    build(strip_lines * first, strip_lines * first + strip_lines + 2, quarter_cols, 2 * quarter_cols)
    center(first)
    pieces[1].wait()
    pieces[2].wait()
    col_edge[0] = lat[pl.ds(1, rows), 8, :]
    col_edge[1] = lat[pl.ds(1, rows), cols + 7, :]
    number = lambda flag: jnp.where(flag, 1, 0)
    vertical = number(up) + number(down)
    horizontal = 1 + number(west) + number(east)
    beside = number(near_west) + number(near_east)
    pl.semaphore_wait(barrier, half_members + vertical * horizontal + beside)
    mirror = (1 - side) * half_members + lax.rem(me, half_members)
    pl.semaphore_signal(side_sem, inc=1, device_id=place(mirror), device_id_type=MESH)

    both = jnp.logical_and
    left_pad, right_pad = pl.ds(0, 8), pl.ds(cols + 8, 8)
    head_cols, tail_cols = pl.ds(0, 8), pl.ds(cols - 8, 8)
    middle = pl.ds(8, cols)
    plan = [
        (west, east, (r, c - 1), col_edge.at[0], col_halo.at[1]),
        (east, west, (r, c + 1), col_edge.at[1], col_halo.at[0]),
        (up, down, (r - 1, c), latent.at[0], lat.at[rows + 1, middle]),
        (down, up, (r + 1, c), latent.at[rows - 1], lat.at[0, middle]),
        (both(up, west), both(down, east), (r - 1, c - 1), latent.at[0, head_cols], lat.at[rows + 1, right_pad]),
        (both(up, east), both(down, west), (r - 1, c + 1), latent.at[0, tail_cols], lat.at[rows + 1, left_pad]),
        (both(down, west), both(up, east), (r + 1, c - 1), latent.at[rows - 1, head_cols], lat.at[0, right_pad]),
        (both(down, east), both(up, west), (r + 1, c + 1), latent.at[rows - 1, tail_cols], lat.at[0, left_pad]),
    ]

    def halo_copy(index):
        _, _, target, source, destination = plan[index]
        return pltpu.make_async_remote_copy(
            src_ref=source, dst_ref=destination, send_sem=halo_send.at[index],
            recv_sem=halo_recv.at[index], device_id=target, device_id_type=MESH,
        )

    def send_halo(indices):
        for index in indices:
            @pl.when(plan[index][0])
            def _(index=index):
                halo_copy(index).start()

    send_halo(range(8))
    send_go(0, first)

    def await_halo(indices):
        for index in indices:
            _, arrives, _, _, destination = plan[index]

            @pl.when(arrives)
            def _(index=index):
                halo_copy(index).wait_recv()

            @pl.when(jnp.logical_not(arrives))
            def _(destination=destination):
                destination[...] = jnp.zeros(destination.shape, F32)

    pieces[3].wait()
    build(third_line, third_line + strip_lines, quarter_cols, 2 * quarter_cols)
    center(third)
    pl.semaphore_wait(side_sem, 1)
    send_go(0, third)
    pieces[4].wait()
    pieces[5].wait()
    await_halo((2, 3))
    outer = 3 * strip_lines + 2
    build(outer * (1 - side), outer * (1 - side) + strip_lines, quarter_cols, 2 * quarter_cols)
    center(second)
    send_go(0, second)
    build(outer * side, outer * side + strip_lines, quarter_cols, 2 * quarter_cols)
    center(fourth)
    send_go(0, fourth)
    recv[0, me] = emb[0, me]

    await_halo((0, 1, 4, 5, 6, 7))
    pieces[6].wait()
    pieces[7].wait()

    def edge(t, carry):
        lat[t + 1, pl.ds(7, 1)] = col_halo[0, pl.ds(t, 1)]
        lat[t + 1, pl.ds(cols + 8, 1)] = col_halo[1, pl.ds(t, 1)]
        return carry

    lax.fori_loop(0, rows, edge, 0)

    def outside(step, carry):
        part = lax.rem(2 * (1 - side + step) + step // 2, 4)
        low = lax.rem(part, 2)
        col = pl.multiple_of(part // 2 * (3 * quarter_cols), quarter_cols)
        line = 4 * strip * low
        build(line, line + 4 * strip + 2, col, quarter_cols)
        embed(1, part, 2 * strip * low, 2 * strip, col, quarter_cols)
        send_go(1, part)
        return carry

    lax.fori_loop(0, 4, outside, 0)
    recv[1, me] = emb[1, me]

    for index in range(4, 11):
        load(index).wait()

    for ref, source in ((wq, w_qkv), (wp, w_proj), (wu, w_up), (wd, w_down)):
        ref[0], ref[1] = split(source[...])

    slot = lax.broadcasted_iota(jnp.int32, (nest, members), 0) // LANES
    number_of = lax.rem(slot, per) * col_count + slot // per
    spread = (number_of == lax.broadcasted_iota(jnp.int32, (nest, members), 1)).astype(F32)
    same = lax.rem(lax.broadcasted_iota(jnp.int32, (nest, nest), 0), LANES) == lax.rem(
        lax.broadcasted_iota(jnp.int32, (nest, nest), 1), LANES
    )
    exact = functools.partial(
        lax.dot_general, precision=lax.Precision.HIGHEST, preferred_element_type=F32
    )

    def widen(h, carry):
        tall = exact(spread, pos_bias[h], (((1,), (0,)), ((), ())))
        bias[h] = jnp.where(same, exact(tall, spread, (((1,), (1,)), ((), ()))), -1e30)
        return carry

    lax.fori_loop(0, HEADS, widen, 0)

    whole = PARTS == 1 or lines == 1
    splits = 1 if whole else lines

    def home(s, owner, part):
        start = owner * share
        if s == 0:
            place_at = out.at[start // (2 * quarter_cols * lines)]
            column = (quarter_cols + lax.rem(start, 2 * quarter_cols)) // groups
            return place_at.at[:, pl.ds(column, runs)] if whole else place_at.at[part, pl.ds(column, runs)]
        row = lax.rem(start, tile_rows * quarter_cols) // quarter_cols
        column = (start // (tile_rows * quarter_cols) * (3 * quarter_cols) + lax.rem(start, quarter_cols)) // groups
        if share <= quarter_cols:
            return out.at[row, :, pl.ds(column, runs)]
        if whole:
            return out.at[pl.ds(row // lines, runs), :, column]
        return out.at[row // lines + part, :, column]

    def ready(s, member, part):
        return done.at[s, member] if whole else done.at[s, member, part]

    def back(s, member, part):
        return pltpu.make_async_remote_copy(
            src_ref=ready(s, member, part), dst_ref=home(s, me, part), send_sem=back_send.at[s, part, member],
            recv_sem=back_recv.at[s, part], device_id=place(member), device_id_type=MESH,
        )

    def own(s, part):
        return pltpu.make_async_copy(ready(s, me, part), home(s, me, part), back_recv.at[s, part])

    lane_head = lax.broadcasted_iota(jnp.int32, (1, lane), 1) // head
    only = [jnp.where(lane_head == h, 1.0, 0.0).astype(BF16) for h in range(lane // head)]
    scale = 1.0 / (head**0.5)

    def block(s, b):
        where = (s, slice(None), b // runs, lax.rem(b, runs))
        rows_of = [where + (slice(first_group, first_group + LANES),) for first_group in range(0, groups, LANES)]
        x = jnp.concatenate([recv[rows_in].reshape(nest, feat) for rows_in in rows_of], axis=0)
        normed = split(layer_norm(x, gain_attn[...]))
        qkv = dot3(normed, (wq[0], wq[1]))
        q = split(qkv[:, :feat] * scale)
        k = split(qkv[:, feat : 2 * feat])
        v = split(qkv[:, 2 * feat :])
        pieces_of = []
        for start in range(0, tokens, nest):
            q_in, k_in, v_in = (tuple(part[start : start + nest] for part in pair) for pair in (q, k, v))
            tiles = []
            for tile in range(0, feat, lane):
                q_tile, k_tile, v_tile = (
                    tuple(part[:, tile : tile + lane] for part in pair) for pair in (q_in, k_in, v_in)
                )
                k_wide = jnp.concatenate([jnp.concatenate([part, part], axis=1) for part in k_tile], axis=0)
                v_line = jnp.concatenate(v_tile, axis=1)
                v_wide = jnp.concatenate([v_line, v_line], axis=0)
                mixed = jnp.zeros((nest, lane), F32)
                for h in range(0, lane // head, pack):
                    heads = range(h, h + pack)
                    q_tall = jnp.concatenate(
                        [jnp.concatenate([part * only[g] for part in q_tile], axis=1) for g in heads], axis=0
                    )
                    products = dot(q_tall, k_wide, ((1,), (1,)))
                    first_head = tile // head + h
                    scores = products[:, :nest] + products[:, nest:] + bias[
                        first_head : first_head + pack
                    ].reshape(pack * nest, nest)
                    expd = jnp.exp(scores - jnp.max(scores, axis=-1, keepdims=True))
                    probs = split(expd * (1.0 / jnp.sum(expd, axis=-1, keepdims=True)))
                    products = dot(jnp.concatenate(probs, axis=1), v_wide)
                    wide = products[:, :lane] + products[:, lane:]
                    for g in heads:
                        mixed = mixed + jnp.where(lane_head == g, wide[(g - h) * nest : (g - h + 1) * nest], 0.0)
                tiles.append(mixed)
            pieces_of.append(jnp.concatenate(tiles, axis=1))
        mixed = jnp.concatenate(pieces_of, axis=0)
        after = x + dot3(split(mixed), (wp[0], wp[1]))
        hidden = gelu(dot3(split(layer_norm(after, gain_mlp[...])), (wu[0], wu[1])))
        result = after + dot3(split(hidden), (wd[0], wd[1]))
        for index, rows_in in enumerate(rows_of):
            done[rows_in] = result[index * nest : (index + 1) * nest].reshape(members, LANES, feat)

    def process(s, carry):
        def await_one(step, inner):
            arrival(s, other(step)).wait_recv()
            return inner

        lax.fori_loop(0, members - 1, await_one, 0)

        def some(part, inner):
            def work(b, inside):
                block(s, b)
                return inside

            count = lines * runs // splits
            lax.fori_loop(part * count, part * count + count, work, 0)

            for stage in range(STAGES):
                @pl.when(s == stage)
                def _(stage=stage):
                    def send(step, inside):
                        back(stage, other(step), part).start()
                        return inside

                    lax.fori_loop(0, members - 1, send, 0)
                    own(stage, part).start()

            return inner

        lax.fori_loop(0, splits, some, 0)
        return carry

    lax.fori_loop(0, STAGES, process, 0)

    for s in range(STAGES):
        def sent(step, carry, s=s):
            member = other(step)
            go(s, member).wait_send()
            for part in range(splits):
                back(s, member, part).wait_send()
            return carry

        lax.fori_loop(0, members - 1, sent, 0)
    for index in range(8):
        @pl.when(plan[index][0])
        def _(index=index):
            halo_copy(index).wait_send()
    for s in range(STAGES):
        for part in range(splits):
            every = done.at[s] if whole else done.at[s, :, part]
            pltpu.make_async_copy(every, every, back_recv.at[s, part]).wait()


def per_device(
    latent, w_small, w_large, gain_embed, gain_attn, w_qkv, pos_bias, w_proj, gain_mlp, w_up, w_down
):
    row_count = lax.axis_size("rows")
    col_count = lax.axis_size("cols")
    samples, rows, cols, chan = latent.shape
    tile_rows, tile_cols = rows // 2, cols // 2
    feat = gain_embed.shape[0]
    half = feat // 2
    members = pos_bias.shape[1]
    phases = row_count // (members // col_count)
    share = tile_rows * tile_cols // STAGES // members
    groups = max(8, min(share, 256 // members))
    pixels = pltpu.VMEM((2, tile_rows + 1, tile_cols, 2 * chan), BF16)
    lines = max(1, share // (tile_cols // 2))
    exchange = pltpu.VMEM((STAGES, members, lines, share // groups // lines, groups, feat), F32)
    dma = pltpu.SemaphoreType.DMA
    inputs = (
        latent[0], w_small, w_large, gain_embed[None], gain_attn[None], w_qkv, pos_bias, w_proj,
        gain_mlp[None], w_up, w_down,
    )
    halves = lambda *shape: pltpu.VMEM((2,) + shape, BF16)
    out_bytes = tile_rows * tile_cols * feat * 4
    out = pl.pallas_call(
        functools.partial(block_kernel, (row_count, col_count, members, phases, groups)),
        name="crossformer_block",
        out_shape=pltpu.VMEM((tile_rows // lines, lines, tile_cols // groups, groups, feat), F32),
        in_specs=[pl.BlockSpec(memory_space=pltpu.HBM)] * 11,
        out_specs=pl.BlockSpec(memory_space=pltpu.VMEM),
        scratch_shapes=[pltpu.VMEM((rows + 2, cols + 16, chan), F32)]
        + [pltpu.VMEM(array.shape, F32) for array in inputs[1:]]
        + [
            pixels, pixels, pixels, pixels,
            halves(2, 2 * chan, feat),
            halves(2, 2 * chan, half),
            halves(4, 2 * chan, half),
            halves(*w_qkv.shape),
            halves(*w_proj.shape),
            halves(*w_up.shape),
            halves(*w_down.shape),
            pltpu.VMEM((HEADS, members * LANES, members * LANES), F32),
            exchange, exchange, exchange,
            pltpu.VMEM((2, rows, chan), F32),
            pltpu.VMEM((2, rows, chan), F32),
            dma((8,)), dma((8,)),
            dma((STAGES, members)), dma((STAGES, members)),
            dma((STAGES, lines, members)), dma((STAGES, lines)),
            dma((11,)), dma((8,)),
            pltpu.SemaphoreType.REGULAR,
        ],
        compiler_params=pltpu.CompilerParams(
            collective_id=0, has_side_effects=True, vmem_limit_bytes=67043328 - out_bytes
        ),
    )(*inputs)
    return out.reshape(samples, tile_rows, tile_cols, feat)


def solution(mesh):
    in_specs = (P(None, "rows", "cols", None),) + (P(),) * 10
    out_specs = P(None, "rows", "cols", None)
    return jax.shard_map(
        per_device, mesh=mesh, in_specs=in_specs, out_specs=out_specs, check_vma=False
    )
```

```python
import functools

import jax
import jax.numpy as jnp
from jax import lax
from jax.experimental import pallas as pl
from jax.experimental.pallas import tpu as pltpu
from jax.sharding import PartitionSpec as P

HEADS = 8
STAGES = 2
PARTS = 2
LANES = 8
MESH = pl.DeviceIdType.MESH
F32 = jnp.float32
BF16 = jnp.bfloat16


def split(values):
    high = values.astype(BF16)
    return high, (values - high.astype(F32)).astype(BF16)


def dot(left, right, dims=((1,), (0,))):
    return lax.dot_general(left, right, (dims, ((), ())), preferred_element_type=F32)


def dot3(left, right, dims=((1,), (0,))):
    left_hi, left_lo = left
    right_hi, right_lo = right
    return (
        dot(left_hi, right_lo, dims) + dot(left_lo, right_hi, dims) + dot(left_hi, right_hi, dims)
    )


def layer_norm(values, gain):
    center = values - jnp.mean(values, axis=-1, keepdims=True)
    spread = jnp.mean(center * center, axis=-1, keepdims=True)
    return center * lax.rsqrt(spread + 1e-05) * gain


def gelu(values):
    return 0.5 * values * (1.0 + lax.erf(values * 0.7071067811865476))


def block_kernel(
    sizes,
    *refs,
):
    inputs, out = refs[:11], refs[11]
    latent = inputs[0]
    (
        lat, w_small, w_large, gain_embed, gain_attn, w_qkv, pos_bias, w_proj, gain_mlp, w_up, w_down,
        eo_hi, eo_lo, oe_hi, oe_lo, wc, we, wo, wq, wp, wu, wd, bias,
        emb, recv, done, col_halo, col_edge,
        halo_send, halo_recv, go_send, go_recv, back_send, back_recv, load_sem, part_sem, side_sem,
    ) = refs[12:]
    loaded = (
        None, w_small, w_large, gain_embed, gain_attn, w_qkv, pos_bias, w_proj, gain_mlp, w_up, w_down,
    )
    row_count, col_count, members, phases, groups = sizes
    rows, cols, chan = latent.shape
    tile_rows, tile_cols = rows // 2, cols // 2
    feat = gain_embed.shape[1]
    half = feat // 2
    quarter_cols = tile_cols // 4
    share = tile_rows * tile_cols // STAGES // members
    lines = max(1, share // (2 * quarter_cols))
    runs = share // groups // lines
    tokens = members * groups
    head = feat // HEADS
    nest = members * LANES
    lane = min(feat, 128)
    pack = min(lane // head, max(1, 1024 // nest))
    half_members = members // 2
    half_cols = col_count // 2
    per = members // col_count
    strip = tile_rows // 4

    r = lax.axis_index("rows")
    c = lax.axis_index("cols")
    core = lax.rem(r, phases)
    side, spot = c // half_cols, lax.rem(c, half_cols)
    band = r // phases
    me = side * half_members + spot * per + band

    def place(member):
        return (
            lax.rem(member, per) * phases + core,
            member // half_members * half_cols + lax.rem(member, half_members) // per,
        )

    def other(step):
        group = step // per
        shift = col_count // 2 + (group + 1) // 2 * (2 * lax.rem(group, 2) - 1)
        to_col = lax.rem(c + shift + col_count, col_count)
        return to_col * per + lax.rem(band + step + 1, per)

    first, fourth = 2 - side, 3 * side
    second, third = 3 - fourth, 3 - first
    left_col, right_col = 2 * quarter_cols - 8, 6 * quarter_cols + 8
    wide = right_col - left_col
    strip_lines = 2 * strip
    third_line = strip_lines * third + 2 * side

    def piece(index, row, row_num, col, col_num):
        return pltpu.make_async_copy(
            latent.at[pl.ds(row, row_num), pl.ds(col, col_num)],
            lat.at[pl.ds(row + 1, row_num), pl.ds(col + 8, col_num)],
            part_sem.at[index],
        )

    pieces = [
        piece(0, strip_lines * first - 1, strip_lines + 2, left_col, wide),
        piece(1, 0, rows, 0, 8),
        piece(2, 0, rows, cols - 8, 8),
        piece(3, third_line - 1, strip_lines, left_col, wide),
        piece(4, 0, strip_lines - 1, left_col, wide),
        piece(5, 3 * strip_lines + 1, strip_lines - 1, left_col, wide),
        piece(6, 0, rows, 8, left_col - 8),
        piece(7, 0, rows, right_col, cols - 8 - right_col),
    ]

    def load(index):
        return pltpu.make_async_copy(inputs[index], loaded[index], load_sem.at[index])

    pieces[0].start()
    load(1).start()
    load(2).start()
    load(3).start()

    barrier = pltpu.get_barrier_semaphore()

    def greet(step, carry):
        opposite = (1 - side) * half_members + lax.rem(me + step, half_members)
        pl.semaphore_signal(barrier, inc=1, device_id=place(opposite), device_id_type=MESH)
        return carry

    lax.fori_loop(0, half_members, greet, 0)
    up, down = r > 0, r < row_count - 1
    west, east = c > 0, c < col_count - 1
    near_west = jnp.logical_and(west, c != half_cols)
    near_east = jnp.logical_and(east, c != half_cols - 1)
    for ok, dc in ((near_west, -1), (near_east, 1)):
        @pl.when(ok)
        def _(dc=dc):
            pl.semaphore_signal(barrier, inc=1, device_id=(r, c + dc), device_id_type=MESH)

    for row_ok, dr in ((up, -1), (down, 1)):
        for col_ok, dc in ((True, 0), (west, -1), (east, 1)):
            ok = row_ok if col_ok is True else jnp.logical_and(row_ok, col_ok)

            @pl.when(ok)
            def _(dr=dr, dc=dc):
                pl.semaphore_signal(barrier, inc=1, device_id=(r + dr, c + dc), device_id_type=MESH)

    for index in range(1, 8):
        pieces[index].start()
    for index in range(4, 11):
        load(index).start()

    def keep(ref, index, values):
        ref[(0,) + index], ref[(1,) + index] = split(values)

    load(1).wait()
    load(2).wait()
    for p in range(2):
        keep(wc, (p, slice(None), slice(0, half)), w_small[2 * p * chan : 2 * (p + 1) * chan])
        start = (p + 1) * 4 * chan + chan
        keep(wc, (p, slice(None), slice(half, feat)), w_large[start : start + 2 * chan])
        start = 3 * p * 4 * chan + chan
        keep(we, (p,), w_large[start : start + 2 * chan])
    for p in range(4):
        keep(wo, (p, slice(0, chan)), w_large[4 * p * chan : (4 * p + 1) * chan])
        keep(wo, (p, slice(chan, 2 * chan)), w_large[(4 * p + 3) * chan : (4 * p + 4) * chan])

    def build(start, stop, col, num):
        area = pl.ds(col, num)

        def line(t, carry):
            b, a = lax.rem(t, 2), t // 2
            for hi, lo, shifts in ((eo_hi, eo_lo, (0, 1)), (oe_hi, oe_lo, (-1, 2))):
                for place_at, shift in zip((slice(0, chan), slice(chan, 2 * chan)), shifts):
                    values = lat[t, pl.ds(8 + 2 * col + shift, num, stride=2), :]
                    hi[b, a, area, place_at], lo[b, a, area, place_at] = split(values)
            return carry

        lax.fori_loop(start, stop, line, 0)

    def go(s, member):
        return pltpu.make_async_remote_copy(
            src_ref=emb.at[s, member], dst_ref=recv.at[s, me], send_sem=go_send.at[s],
            recv_sem=go_recv.at[s], device_id=place(member), device_id_type=MESH,
        )

    def embed(s, part, row, row_num, col, col_num):
        def taps(hi, lo, p):
            where = (p % 2, pl.ds(row + p // 2, row_num), pl.ds(col, col_num))
            return tuple(ref[where].reshape(row_num * col_num, 2 * chan) for ref in (hi, lo))

        def pair(ref, index):
            return ref[0, index], ref[1, index]

        wide = dot3(taps(eo_hi, eo_lo, 1), pair(wc, 0)) + dot3(taps(eo_hi, eo_lo, 2), pair(wc, 1))
        thin = dot3(taps(eo_hi, eo_lo, 0), pair(we, 0)) + dot3(taps(eo_hi, eo_lo, 3), pair(we, 1))
        for p in range(4):
            thin = thin + dot3(taps(oe_hi, oe_lo, p), pair(wo, p))
        joined = jnp.concatenate([wide[:, :half], wide[:, half:] + thin], axis=-1)
        emb[s, pl.ds(part * (members // 4), members // 4)] = layer_norm(joined, gain_embed[...]).reshape(
            members // 4, lines, runs, groups, feat
        )

    def send_go(s, part):
        def send(step, carry):
            member = part * (members // 4) + lax.rem(me + step, members // 4)

            @pl.when(member != me)
            def _():
                go(s, member).start()

            return carry

        lax.fori_loop(0, members // 4, send, 0)

    pieces[0].wait()
    load(3).wait()
    def center(part):
        embed(0, part, strip * part, strip, quarter_cols, 2 * quarter_cols)

    build(strip_lines * first, strip_lines * first + strip_lines + 2, quarter_cols, 2 * quarter_cols)
    center(first)
    pieces[1].wait()
    pieces[2].wait()
    col_edge[0] = lat[pl.ds(1, rows), 8, :]
    col_edge[1] = lat[pl.ds(1, rows), cols + 7, :]
    number = lambda flag: jnp.where(flag, 1, 0)
    vertical = number(up) + number(down)
    horizontal = 1 + number(west) + number(east)
    beside = number(near_west) + number(near_east)
    pl.semaphore_wait(barrier, half_members + vertical * horizontal + beside)
    mirror = (1 - side) * half_members + lax.rem(me, half_members)
    pl.semaphore_signal(side_sem, inc=1, device_id=place(mirror), device_id_type=MESH)

    both = jnp.logical_and
    left_pad, right_pad = pl.ds(0, 8), pl.ds(cols + 8, 8)
    head_cols, tail_cols = pl.ds(0, 8), pl.ds(cols - 8, 8)
    middle = pl.ds(8, cols)
    plan = [
        (west, east, (r, c - 1), col_edge.at[0], col_halo.at[1]),
        (east, west, (r, c + 1), col_edge.at[1], col_halo.at[0]),
        (up, down, (r - 1, c), latent.at[0], lat.at[rows + 1, middle]),
        (down, up, (r + 1, c), latent.at[rows - 1], lat.at[0, middle]),
        (both(up, west), both(down, east), (r - 1, c - 1), latent.at[0, head_cols], lat.at[rows + 1, right_pad]),
        (both(up, east), both(down, west), (r - 1, c + 1), latent.at[0, tail_cols], lat.at[rows + 1, left_pad]),
        (both(down, west), both(up, east), (r + 1, c - 1), latent.at[rows - 1, head_cols], lat.at[0, right_pad]),
        (both(down, east), both(up, west), (r + 1, c + 1), latent.at[rows - 1, tail_cols], lat.at[0, left_pad]),
    ]

    def halo_copy(index):
        _, _, target, source, destination = plan[index]
        return pltpu.make_async_remote_copy(
            src_ref=source, dst_ref=destination, send_sem=halo_send.at[index],
            recv_sem=halo_recv.at[index], device_id=target, device_id_type=MESH,
        )

    def send_halo(indices):
        for index in indices:
            @pl.when(plan[index][0])
            def _(index=index):
                halo_copy(index).start()

    send_halo(range(8))
    send_go(0, first)

    def await_halo(indices):
        for index in indices:
            _, arrives, _, _, destination = plan[index]

            @pl.when(arrives)
            def _(index=index):
                halo_copy(index).wait_recv()

            @pl.when(jnp.logical_not(arrives))
            def _(destination=destination):
                destination[...] = jnp.zeros(destination.shape, F32)

    pieces[3].wait()
    build(third_line, third_line + strip_lines, quarter_cols, 2 * quarter_cols)
    center(third)
    pl.semaphore_wait(side_sem, 1)
    send_go(0, third)
    pieces[4].wait()
    pieces[5].wait()
    await_halo((2, 3))
    outer = 3 * strip_lines + 2
    build(outer * (1 - side), outer * (1 - side) + strip_lines, quarter_cols, 2 * quarter_cols)
    center(second)
    send_go(0, second)
    build(outer * side, outer * side + strip_lines, quarter_cols, 2 * quarter_cols)
    center(fourth)
    send_go(0, fourth)
    recv[0, me] = emb[0, me]

    await_halo((0, 1, 4, 5, 6, 7))
    pieces[6].wait()
    pieces[7].wait()

    def edge(t, carry):
        lat[t + 1, pl.ds(7, 1)] = col_halo[0, pl.ds(t, 1)]
        lat[t + 1, pl.ds(cols + 8, 1)] = col_halo[1, pl.ds(t, 1)]
        return carry

    lax.fori_loop(0, rows, edge, 0)

    def outside(step, carry):
        part = lax.rem(2 * (1 - side + step) + step // 2, 4)
        low = lax.rem(part, 2)
        col = pl.multiple_of(part // 2 * (3 * quarter_cols), quarter_cols)
        line = 4 * strip * low
        build(line, line + 4 * strip + 2, col, quarter_cols)
        embed(1, part, 2 * strip * low, 2 * strip, col, quarter_cols)
        send_go(1, part)
        return carry

    lax.fori_loop(0, 4, outside, 0)
    recv[1, me] = emb[1, me]

    for index in range(4, 11):
        load(index).wait()

    for ref, source in ((wq, w_qkv), (wp, w_proj), (wu, w_up), (wd, w_down)):
        ref[0], ref[1] = split(source[...])

    slot = lax.broadcasted_iota(jnp.int32, (nest, members), 0) // LANES
    number_of = lax.rem(slot, per) * col_count + slot // per
    spread = (number_of == lax.broadcasted_iota(jnp.int32, (nest, members), 1)).astype(F32)
    same = lax.rem(lax.broadcasted_iota(jnp.int32, (nest, nest), 0), LANES) == lax.rem(
        lax.broadcasted_iota(jnp.int32, (nest, nest), 1), LANES
    )
    exact = functools.partial(
        lax.dot_general, precision=lax.Precision.HIGHEST, preferred_element_type=F32
    )

    def widen(h, carry):
        tall = exact(spread, pos_bias[h], (((1,), (0,)), ((), ())))
        bias[h] = jnp.where(same, exact(tall, spread, (((1,), (1,)), ((), ()))), -1e30)
        return carry

    lax.fori_loop(0, HEADS, widen, 0)

    whole = PARTS == 1 or lines == 1
    splits = 1 if whole else lines

    def home(s, owner, part):
        start = owner * share
        if s == 0:
            place_at = out.at[start // (2 * quarter_cols * lines)]
            column = (quarter_cols + lax.rem(start, 2 * quarter_cols)) // groups
            return place_at.at[:, pl.ds(column, runs)] if whole else place_at.at[part, pl.ds(column, runs)]
        row = lax.rem(start, tile_rows * quarter_cols) // quarter_cols
        column = (start // (tile_rows * quarter_cols) * (3 * quarter_cols) + lax.rem(start, quarter_cols)) // groups
        if share <= quarter_cols:
            return out.at[row, :, pl.ds(column, runs)]
        if whole:
            return out.at[pl.ds(row // lines, runs), :, column]
        return out.at[row // lines + part, :, column]

    def ready(s, member, part):
        return done.at[s, member] if whole else done.at[s, member, part]

    def back(s, member, part):
        return pltpu.make_async_remote_copy(
            src_ref=ready(s, member, part), dst_ref=home(s, me, part), send_sem=back_send.at[s, part],
            recv_sem=back_recv.at[s, part], device_id=place(member), device_id_type=MESH,
        )

    def own(s, part):
        return pltpu.make_async_copy(ready(s, me, part), home(s, me, part), back_recv.at[s, part])

    lane_head = lax.broadcasted_iota(jnp.int32, (1, lane), 1) // head
    only = [jnp.where(lane_head == h, 1.0, 0.0).astype(BF16) for h in range(lane // head)]
    scale = 1.0 / (head**0.5)

    def block(s, b):
        where = (s, slice(None), b // runs, lax.rem(b, runs))
        rows_of = [where + (slice(first_group, first_group + LANES),) for first_group in range(0, groups, LANES)]
        x = jnp.concatenate([recv[rows_in].reshape(nest, feat) for rows_in in rows_of], axis=0)
        normed = split(layer_norm(x, gain_attn[...]))
        qkv = dot3(normed, (wq[0], wq[1]))
        q = split(qkv[:, :feat] * scale)
        k = split(qkv[:, feat : 2 * feat])
        v = split(qkv[:, 2 * feat :])
        pieces_of = []
        for start in range(0, tokens, nest):
            q_in, k_in, v_in = (tuple(part[start : start + nest] for part in pair) for pair in (q, k, v))
            tiles = []
            for tile in range(0, feat, lane):
                q_tile, k_tile, v_tile = (
                    tuple(part[:, tile : tile + lane] for part in pair) for pair in (q_in, k_in, v_in)
                )
                k_wide = jnp.concatenate([jnp.concatenate([part, part], axis=1) for part in k_tile], axis=0)
                v_line = jnp.concatenate(v_tile, axis=1)
                v_wide = jnp.concatenate([v_line, v_line], axis=0)
                mixed = jnp.zeros((nest, lane), F32)
                for h in range(0, lane // head, pack):
                    heads = range(h, h + pack)
                    q_tall = jnp.concatenate(
                        [jnp.concatenate([part * only[g] for part in q_tile], axis=1) for g in heads], axis=0
                    )
                    products = dot(q_tall, k_wide, ((1,), (1,)))
                    first_head = tile // head + h
                    scores = products[:, :nest] + products[:, nest:] + bias[
                        first_head : first_head + pack
                    ].reshape(pack * nest, nest)
                    expd = jnp.exp(scores - jnp.max(scores, axis=-1, keepdims=True))
                    probs = split(expd * (1.0 / jnp.sum(expd, axis=-1, keepdims=True)))
                    products = dot(jnp.concatenate(probs, axis=1), v_wide)
                    wide = products[:, :lane] + products[:, lane:]
                    for g in heads:
                        mixed = mixed + jnp.where(lane_head == g, wide[(g - h) * nest : (g - h + 1) * nest], 0.0)
                tiles.append(mixed)
            pieces_of.append(jnp.concatenate(tiles, axis=1))
        mixed = jnp.concatenate(pieces_of, axis=0)
        after = x + dot3(split(mixed), (wp[0], wp[1]))
        hidden = gelu(dot3(split(layer_norm(after, gain_mlp[...])), (wu[0], wu[1])))
        result = after + dot3(split(hidden), (wd[0], wd[1]))
        for index, rows_in in enumerate(rows_of):
            done[rows_in] = result[index * nest : (index + 1) * nest].reshape(members, LANES, feat)

    def process(s, carry):
        rest = pl.ds(0, members - 1)
        pltpu.make_async_copy(emb.at[s, rest], recv.at[s, rest], go_recv.at[s]).wait()

        def some(part, inner):
            def work(b, inside):
                block(s, b)
                return inside

            count = lines * runs // splits
            lax.fori_loop(part * count, part * count + count, work, 0)

            for stage in range(STAGES):
                @pl.when(s == stage)
                def _(stage=stage):
                    def send(step, inside):
                        back(stage, other(step), part).start()
                        return inside

                    lax.fori_loop(0, members - 1, send, 0)
                    own(stage, part).start()

            return inner

        lax.fori_loop(0, splits, some, 0)
        return carry

    lax.fori_loop(0, STAGES, process, 0)

    for s in range(STAGES):
        rest = pl.ds(0, members - 1)
        pltpu.make_async_copy(emb.at[s, rest], recv.at[s, rest], go_send.at[s]).wait()
        for part in range(splits):
            others = done.at[s, rest] if whole else done.at[s, rest, part]
            pltpu.make_async_copy(others, others, back_send.at[s, part]).wait()
    for index in range(8):
        @pl.when(plan[index][0])
        def _(index=index):
            halo_copy(index).wait_send()
    for s in range(STAGES):
        for part in range(splits):
            every = done.at[s] if whole else done.at[s, :, part]
            pltpu.make_async_copy(every, every, back_recv.at[s, part]).wait()


def per_device(
    latent, w_small, w_large, gain_embed, gain_attn, w_qkv, pos_bias, w_proj, gain_mlp, w_up, w_down
):
    row_count = lax.axis_size("rows")
    col_count = lax.axis_size("cols")
    samples, rows, cols, chan = latent.shape
    tile_rows, tile_cols = rows // 2, cols // 2
    feat = gain_embed.shape[0]
    half = feat // 2
    members = pos_bias.shape[1]
    phases = row_count // (members // col_count)
    share = tile_rows * tile_cols // STAGES // members
    groups = max(8, min(share, 256 // members))
    pixels = pltpu.VMEM((2, tile_rows + 1, tile_cols, 2 * chan), BF16)
    lines = max(1, share // (tile_cols // 2))
    exchange = pltpu.VMEM((STAGES, members, lines, share // groups // lines, groups, feat), F32)
    dma = pltpu.SemaphoreType.DMA
    inputs = (
        latent[0], w_small, w_large, gain_embed[None], gain_attn[None], w_qkv, pos_bias, w_proj,
        gain_mlp[None], w_up, w_down,
    )
    halves = lambda *shape: pltpu.VMEM((2,) + shape, BF16)
    out_bytes = tile_rows * tile_cols * feat * 4
    out = pl.pallas_call(
        functools.partial(block_kernel, (row_count, col_count, members, phases, groups)),
        name="crossformer_block",
        out_shape=pltpu.VMEM((tile_rows // lines, lines, tile_cols // groups, groups, feat), F32),
        in_specs=[pl.BlockSpec(memory_space=pltpu.HBM)] * 11,
        out_specs=pl.BlockSpec(memory_space=pltpu.VMEM),
        scratch_shapes=[pltpu.VMEM((rows + 2, cols + 16, chan), F32)]
        + [pltpu.VMEM(array.shape, F32) for array in inputs[1:]]
        + [
            pixels, pixels, pixels, pixels,
            halves(2, 2 * chan, feat),
            halves(2, 2 * chan, half),
            halves(4, 2 * chan, half),
            halves(*w_qkv.shape),
            halves(*w_proj.shape),
            halves(*w_up.shape),
            halves(*w_down.shape),
            pltpu.VMEM((HEADS, members * LANES, members * LANES), F32),
            exchange, exchange, exchange,
            pltpu.VMEM((2, rows, chan), F32),
            pltpu.VMEM((2, rows, chan), F32),
            dma((8,)), dma((8,)),
            dma((STAGES,)), dma((STAGES,)),
            dma((STAGES, lines)), dma((STAGES, lines)),
            dma((11,)), dma((8,)),
            pltpu.SemaphoreType.REGULAR,
        ],
        compiler_params=pltpu.CompilerParams(
            collective_id=0, has_side_effects=True, vmem_limit_bytes=67043328 - out_bytes
        ),
    )(*inputs)
    return out.reshape(samples, tile_rows, tile_cols, feat)


def solution(mesh):
    in_specs = (P(None, "rows", "cols", None),) + (P(),) * 10
    out_specs = P(None, "rows", "cols", None)
    return jax.shard_map(
        per_device, mesh=mesh, in_specs=in_specs, out_specs=out_specs, check_vma=False
    )
```

```python
import functools

import jax
import jax.numpy as jnp
from jax import lax
from jax.experimental import pallas as pl
from jax.experimental.pallas import tpu as pltpu
from jax.sharding import PartitionSpec as P

HEADS = 8
STAGES = 2
PARTS = 2
LANES = 8
MESH = pl.DeviceIdType.MESH
F32 = jnp.float32
BF16 = jnp.bfloat16


def split(values):
    high = values.astype(BF16)
    return high, (values - high.astype(F32)).astype(BF16)


def dot(left, right, dims=((1,), (0,))):
    return lax.dot_general(left, right, (dims, ((), ())), preferred_element_type=F32)


def dot3(left, right, dims=((1,), (0,))):
    left_hi, left_lo = left
    right_hi, right_lo = right
    return (
        dot(left_hi, right_lo, dims) + dot(left_lo, right_hi, dims) + dot(left_hi, right_hi, dims)
    )


def layer_norm(values, gain):
    center = values - jnp.mean(values, axis=-1, keepdims=True)
    spread = jnp.mean(center * center, axis=-1, keepdims=True)
    return center * lax.rsqrt(spread + 1e-05) * gain


def gelu(values):
    return 0.5 * values * (1.0 + lax.erf(values * 0.7071067811865476))


def block_kernel(
    sizes,
    *refs,
):
    inputs, out = refs[:11], refs[11]
    latent = inputs[0]
    (
        lat, w_small, w_large, gain_embed, gain_attn, w_qkv, pos_bias, w_proj, gain_mlp, w_up, w_down,
        eo_hi, eo_lo, oe_hi, oe_lo, wc, we, wo, wq, wp, wu, wd, bias,
        emb, recv, done, col_halo, col_edge,
        halo_send, halo_recv, go_send, go_recv, back_send, back_recv, load_sem, part_sem, side_sem,
    ) = refs[12:]
    loaded = (
        None, w_small, w_large, gain_embed, gain_attn, w_qkv, pos_bias, w_proj, gain_mlp, w_up, w_down,
    )
    row_count, col_count, members, phases, groups = sizes
    rows, cols, chan = latent.shape
    tile_rows, tile_cols = rows // 2, cols // 2
    feat = gain_embed.shape[1]
    half = feat // 2
    quarter_cols = tile_cols // 4
    share = tile_rows * tile_cols // STAGES // members
    lines = max(1, share // (2 * quarter_cols))
    runs = share // groups // lines
    tokens = members * groups
    head = feat // HEADS
    nest = members * LANES
    lane = min(feat, 128)
    pack = min(lane // head, max(1, 1024 // nest))
    half_members = members // 2
    half_cols = col_count // 2
    per = members // col_count
    strip = tile_rows // 4

    r = lax.axis_index("rows")
    c = lax.axis_index("cols")
    core = lax.rem(r, phases)
    side, spot = c // half_cols, lax.rem(c, half_cols)
    band = r // phases
    me = side * half_members + spot * per + band

    def place(member):
        return (
            lax.rem(member, per) * phases + core,
            member // half_members * half_cols + lax.rem(member, half_members) // per,
        )

    def other(step):
        group = step // per
        shift = col_count // 2 + (group + 1) // 2 * (2 * lax.rem(group, 2) - 1)
        to_col = lax.rem(c + shift + col_count, col_count)
        return to_col * per + lax.rem(band + step + 1, per)

    first, fourth = 2 - side, 3 * side
    second, third = 3 - fourth, 3 - first
    left_col, right_col = 2 * quarter_cols - 8, 6 * quarter_cols + 8
    wide = right_col - left_col
    strip_lines = 2 * strip
    third_line = strip_lines * third + 2 * side

    def piece(index, row, row_num, col, col_num):
        return pltpu.make_async_copy(
            latent.at[pl.ds(row, row_num), pl.ds(col, col_num)],
            lat.at[pl.ds(row + 1, row_num), pl.ds(col + 8, col_num)],
            part_sem.at[index],
        )

    pieces = [
        piece(0, strip_lines * first - 1, strip_lines + 2, left_col, wide),
        piece(1, 0, rows, 0, 8),
        piece(2, 0, rows, cols - 8, 8),
        piece(3, third_line - 1, strip_lines, left_col, wide),
        piece(4, 0, strip_lines - 1, left_col, wide),
        piece(5, 3 * strip_lines + 1, strip_lines - 1, left_col, wide),
        piece(6, 0, rows, 8, left_col - 8),
        piece(7, 0, rows, right_col, cols - 8 - right_col),
    ]

    def load(index):
        return pltpu.make_async_copy(inputs[index], loaded[index], load_sem.at[index])

    pieces[0].start()
    load(1).start()
    load(2).start()
    load(3).start()

    barrier = pltpu.get_barrier_semaphore()

    def greet(step, carry):
        opposite = (1 - side) * half_members + lax.rem(me + step, half_members)
        pl.semaphore_signal(barrier, inc=1, device_id=place(opposite), device_id_type=MESH)
        return carry

    lax.fori_loop(0, half_members, greet, 0)
    up, down = r > 0, r < row_count - 1
    west, east = c > 0, c < col_count - 1
    near_west = jnp.logical_and(west, c != half_cols)
    near_east = jnp.logical_and(east, c != half_cols - 1)
    for ok, dc in ((near_west, -1), (near_east, 1)):
        @pl.when(ok)
        def _(dc=dc):
            pl.semaphore_signal(barrier, inc=1, device_id=(r, c + dc), device_id_type=MESH)

    for row_ok, dr in ((up, -1), (down, 1)):
        for col_ok, dc in ((True, 0), (west, -1), (east, 1)):
            ok = row_ok if col_ok is True else jnp.logical_and(row_ok, col_ok)

            @pl.when(ok)
            def _(dr=dr, dc=dc):
                pl.semaphore_signal(barrier, inc=1, device_id=(r + dr, c + dc), device_id_type=MESH)

    for index in range(1, 8):
        pieces[index].start()
    for index in range(4, 11):
        load(index).start()

    def keep(ref, index, values):
        ref[(0,) + index], ref[(1,) + index] = split(values)

    load(1).wait()
    load(2).wait()
    for p in range(2):
        keep(wc, (p, slice(None), slice(0, half)), w_small[2 * p * chan : 2 * (p + 1) * chan])
        start = (p + 1) * 4 * chan + chan
        keep(wc, (p, slice(None), slice(half, feat)), w_large[start : start + 2 * chan])
        start = 3 * p * 4 * chan + chan
        keep(we, (p,), w_large[start : start + 2 * chan])
    for p in range(4):
        keep(wo, (p, slice(0, chan)), w_large[4 * p * chan : (4 * p + 1) * chan])
        keep(wo, (p, slice(chan, 2 * chan)), w_large[(4 * p + 3) * chan : (4 * p + 4) * chan])

    def build(start, stop, col, num):
        area = pl.ds(col, num)

        def line(t, carry):
            b, a = lax.rem(t, 2), t // 2
            for hi, lo, shifts in ((eo_hi, eo_lo, (0, 1)), (oe_hi, oe_lo, (-1, 2))):
                for place_at, shift in zip((slice(0, chan), slice(chan, 2 * chan)), shifts):
                    values = lat[t, pl.ds(8 + 2 * col + shift, num, stride=2), :]
                    hi[b, a, area, place_at], lo[b, a, area, place_at] = split(values)
            return carry

        lax.fori_loop(start, stop, line, 0)

    def go(s, member):
        return pltpu.make_async_remote_copy(
            src_ref=emb.at[s, member], dst_ref=recv.at[s, me], send_sem=go_send.at[s],
            recv_sem=go_recv.at[s], device_id=place(member), device_id_type=MESH,
        )

    def embed(s, part, row, row_num, col, col_num):
        def taps(hi, lo, p):
            where = (p % 2, pl.ds(row + p // 2, row_num), pl.ds(col, col_num))
            return tuple(ref[where].reshape(row_num * col_num, 2 * chan) for ref in (hi, lo))

        def pair(ref, index):
            return ref[0, index], ref[1, index]

        wide = dot3(taps(eo_hi, eo_lo, 1), pair(wc, 0)) + dot3(taps(eo_hi, eo_lo, 2), pair(wc, 1))
        def both_halves(hi, lo, p, ref, index):
            tall = jnp.concatenate(taps(hi, lo, p), axis=0)
            return dot(tall, jnp.concatenate(pair(ref, index), axis=1))

        packed = both_halves(eo_hi, eo_lo, 0, we, 0) + both_halves(eo_hi, eo_lo, 3, we, 1)
        for p in range(4):
            packed = packed + both_halves(oe_hi, oe_lo, p, wo, p)
        count = row_num * col_num
        thin = packed[:count, :half] + (packed[:count, half:] + packed[count:, :half])
        joined = jnp.concatenate([wide[:, :half], wide[:, half:] + thin], axis=-1)
        emb[s, pl.ds(part * (members // 4), members // 4)] = layer_norm(joined, gain_embed[...]).reshape(
            members // 4, lines, runs, groups, feat
        )

    def send_go(s, part):
        def send(step, carry):
            member = part * (members // 4) + lax.rem(me + step, members // 4)

            @pl.when(member != me)
            def _():
                go(s, member).start()

            return carry

        lax.fori_loop(0, members // 4, send, 0)

    pieces[0].wait()
    load(3).wait()
    def center(part):
        embed(0, part, strip * part, strip, quarter_cols, 2 * quarter_cols)

    build(strip_lines * first, strip_lines * first + strip_lines + 2, quarter_cols, 2 * quarter_cols)
    center(first)
    pieces[1].wait()
    pieces[2].wait()
    col_edge[0] = lat[pl.ds(1, rows), 8, :]
    col_edge[1] = lat[pl.ds(1, rows), cols + 7, :]
    number = lambda flag: jnp.where(flag, 1, 0)
    vertical = number(up) + number(down)
    horizontal = 1 + number(west) + number(east)
    beside = number(near_west) + number(near_east)
    pl.semaphore_wait(barrier, half_members + vertical * horizontal + beside)
    mirror = (1 - side) * half_members + lax.rem(me, half_members)
    pl.semaphore_signal(side_sem, inc=1, device_id=place(mirror), device_id_type=MESH)

    both = jnp.logical_and
    left_pad, right_pad = pl.ds(0, 8), pl.ds(cols + 8, 8)
    head_cols, tail_cols = pl.ds(0, 8), pl.ds(cols - 8, 8)
    middle = pl.ds(8, cols)
    plan = [
        (west, east, (r, c - 1), col_edge.at[0], col_halo.at[1]),
        (east, west, (r, c + 1), col_edge.at[1], col_halo.at[0]),
        (up, down, (r - 1, c), latent.at[0], lat.at[rows + 1, middle]),
        (down, up, (r + 1, c), latent.at[rows - 1], lat.at[0, middle]),
        (both(up, west), both(down, east), (r - 1, c - 1), latent.at[0, head_cols], lat.at[rows + 1, right_pad]),
        (both(up, east), both(down, west), (r - 1, c + 1), latent.at[0, tail_cols], lat.at[rows + 1, left_pad]),
        (both(down, west), both(up, east), (r + 1, c - 1), latent.at[rows - 1, head_cols], lat.at[0, right_pad]),
        (both(down, east), both(up, west), (r + 1, c + 1), latent.at[rows - 1, tail_cols], lat.at[0, left_pad]),
    ]

    def halo_copy(index):
        _, _, target, source, destination = plan[index]
        return pltpu.make_async_remote_copy(
            src_ref=source, dst_ref=destination, send_sem=halo_send.at[index],
            recv_sem=halo_recv.at[index], device_id=target, device_id_type=MESH,
        )

    def send_halo(indices):
        for index in indices:
            @pl.when(plan[index][0])
            def _(index=index):
                halo_copy(index).start()

    send_halo(range(8))
    send_go(0, first)

    def await_halo(indices):
        for index in indices:
            _, arrives, _, _, destination = plan[index]

            @pl.when(arrives)
            def _(index=index):
                halo_copy(index).wait_recv()

            @pl.when(jnp.logical_not(arrives))
            def _(destination=destination):
                destination[...] = jnp.zeros(destination.shape, F32)

    pieces[3].wait()
    build(third_line, third_line + strip_lines, quarter_cols, 2 * quarter_cols)
    center(third)
    pl.semaphore_wait(side_sem, 1)
    send_go(0, third)
    pieces[4].wait()
    pieces[5].wait()
    await_halo((2, 3))
    outer = 3 * strip_lines + 2
    build(outer * (1 - side), outer * (1 - side) + strip_lines, quarter_cols, 2 * quarter_cols)
    center(second)
    send_go(0, second)
    build(outer * side, outer * side + strip_lines, quarter_cols, 2 * quarter_cols)
    center(fourth)
    send_go(0, fourth)
    recv[0, me] = emb[0, me]

    await_halo((0, 1, 4, 5, 6, 7))
    pieces[6].wait()
    pieces[7].wait()

    def edge(t, carry):
        lat[t + 1, pl.ds(7, 1)] = col_halo[0, pl.ds(t, 1)]
        lat[t + 1, pl.ds(cols + 8, 1)] = col_halo[1, pl.ds(t, 1)]
        return carry

    lax.fori_loop(0, rows, edge, 0)

    def outside(step, carry):
        part = lax.rem(2 * (1 - side + step) + step // 2, 4)
        low = lax.rem(part, 2)
        col = pl.multiple_of(part // 2 * (3 * quarter_cols), quarter_cols)
        line = 4 * strip * low
        build(line, line + 4 * strip + 2, col, quarter_cols)
        embed(1, part, 2 * strip * low, 2 * strip, col, quarter_cols)
        send_go(1, part)
        return carry

    lax.fori_loop(0, 4, outside, 0)
    recv[1, me] = emb[1, me]

    for index in range(4, 11):
        load(index).wait()

    for ref, source in ((wq, w_qkv), (wp, w_proj), (wu, w_up), (wd, w_down)):
        ref[0], ref[1] = split(source[...])

    slot = lax.broadcasted_iota(jnp.int32, (nest, members), 0) // LANES
    number_of = lax.rem(slot, per) * col_count + slot // per
    spread = (number_of == lax.broadcasted_iota(jnp.int32, (nest, members), 1)).astype(F32)
    same = lax.rem(lax.broadcasted_iota(jnp.int32, (nest, nest), 0), LANES) == lax.rem(
        lax.broadcasted_iota(jnp.int32, (nest, nest), 1), LANES
    )
    exact = functools.partial(
        lax.dot_general, precision=lax.Precision.HIGHEST, preferred_element_type=F32
    )

    def widen(h, carry):
        tall = exact(spread, pos_bias[h], (((1,), (0,)), ((), ())))
        bias[h] = jnp.where(same, exact(tall, spread, (((1,), (1,)), ((), ()))), -1e30)
        return carry

    lax.fori_loop(0, HEADS, widen, 0)

    whole = PARTS == 1 or lines == 1
    splits = 1 if whole else lines

    def home(s, owner, part):
        start = owner * share
        if s == 0:
            place_at = out.at[start // (2 * quarter_cols * lines)]
            column = (quarter_cols + lax.rem(start, 2 * quarter_cols)) // groups
            return place_at.at[:, pl.ds(column, runs)] if whole else place_at.at[part, pl.ds(column, runs)]
        row = lax.rem(start, tile_rows * quarter_cols) // quarter_cols
        column = (start // (tile_rows * quarter_cols) * (3 * quarter_cols) + lax.rem(start, quarter_cols)) // groups
        if share <= quarter_cols:
            return out.at[row, :, pl.ds(column, runs)]
        if whole:
            return out.at[pl.ds(row // lines, runs), :, column]
        return out.at[row // lines + part, :, column]

    def ready(s, member, part):
        return done.at[s, member] if whole else done.at[s, member, part]

    def back(s, member, part):
        return pltpu.make_async_remote_copy(
            src_ref=ready(s, member, part), dst_ref=home(s, me, part), send_sem=back_send.at[s, part],
            recv_sem=back_recv.at[s, part], device_id=place(member), device_id_type=MESH,
        )

    def own(s, part):
        return pltpu.make_async_copy(ready(s, me, part), home(s, me, part), back_recv.at[s, part])

    lane_head = lax.broadcasted_iota(jnp.int32, (1, lane), 1) // head
    only = [jnp.where(lane_head == h, 1.0, 0.0).astype(BF16) for h in range(lane // head)]
    scale = 1.0 / (head**0.5)

    def block(s, b):
        where = (s, slice(None), b // runs, lax.rem(b, runs))
        rows_of = [where + (slice(first_group, first_group + LANES),) for first_group in range(0, groups, LANES)]
        x = jnp.concatenate([recv[rows_in].reshape(nest, feat) for rows_in in rows_of], axis=0)
        normed = split(layer_norm(x, gain_attn[...]))
        qkv = dot3(normed, (wq[0], wq[1]))
        q = split(qkv[:, :feat] * scale)
        k = split(qkv[:, feat : 2 * feat])
        v = split(qkv[:, 2 * feat :])
        pieces_of = []
        for start in range(0, tokens, nest):
            q_in, k_in, v_in = (tuple(part[start : start + nest] for part in pair) for pair in (q, k, v))
            tiles = []
            for tile in range(0, feat, lane):
                q_tile, k_tile, v_tile = (
                    tuple(part[:, tile : tile + lane] for part in pair) for pair in (q_in, k_in, v_in)
                )
                k_wide = jnp.concatenate([jnp.concatenate([part, part], axis=1) for part in k_tile], axis=0)
                v_line = jnp.concatenate(v_tile, axis=1)
                v_wide = jnp.concatenate([v_line, v_line], axis=0)
                mixed = jnp.zeros((nest, lane), F32)
                for h in range(0, lane // head, pack):
                    heads = range(h, h + pack)
                    q_tall = jnp.concatenate(
                        [jnp.concatenate([part * only[g] for part in q_tile], axis=1) for g in heads], axis=0
                    )
                    products = dot(q_tall, k_wide, ((1,), (1,)))
                    first_head = tile // head + h
                    scores = products[:, :nest] + products[:, nest:] + bias[
                        first_head : first_head + pack
                    ].reshape(pack * nest, nest)
                    expd = jnp.exp(scores - jnp.max(scores, axis=-1, keepdims=True))
                    probs = split(expd * (1.0 / jnp.sum(expd, axis=-1, keepdims=True)))
                    products = dot(jnp.concatenate(probs, axis=1), v_wide)
                    wide = products[:, :lane] + products[:, lane:]
                    for g in heads:
                        mixed = mixed + jnp.where(lane_head == g, wide[(g - h) * nest : (g - h + 1) * nest], 0.0)
                tiles.append(mixed)
            pieces_of.append(jnp.concatenate(tiles, axis=1))
        mixed = jnp.concatenate(pieces_of, axis=0)
        after = x + dot3(split(mixed), (wp[0], wp[1]))
        hidden = gelu(dot3(split(layer_norm(after, gain_mlp[...])), (wu[0], wu[1])))
        result = after + dot3(split(hidden), (wd[0], wd[1]))
        for index, rows_in in enumerate(rows_of):
            done[rows_in] = result[index * nest : (index + 1) * nest].reshape(members, LANES, feat)

    def process(s, carry):
        rest = pl.ds(0, members - 1)
        pltpu.make_async_copy(emb.at[s, rest], recv.at[s, rest], go_recv.at[s]).wait()

        def some(part, inner):
            def work(b, inside):
                block(s, b)
                return inside

            count = lines * runs // splits
            lax.fori_loop(part * count, part * count + count, work, 0)

            for stage in range(STAGES):
                @pl.when(s == stage)
                def _(stage=stage):
                    def send(step, inside):
                        back(stage, other(step), part).start()
                        return inside

                    lax.fori_loop(0, members - 1, send, 0)
                    own(stage, part).start()

            return inner

        lax.fori_loop(0, splits, some, 0)
        return carry

    lax.fori_loop(0, STAGES, process, 0)

    for s in range(STAGES):
        rest = pl.ds(0, members - 1)
        pltpu.make_async_copy(emb.at[s, rest], recv.at[s, rest], go_send.at[s]).wait()
        for part in range(splits):
            others = done.at[s, rest] if whole else done.at[s, rest, part]
            pltpu.make_async_copy(others, others, back_send.at[s, part]).wait()
    for index in range(8):
        @pl.when(plan[index][0])
        def _(index=index):
            halo_copy(index).wait_send()
    for s in range(STAGES):
        for part in range(splits):
            every = done.at[s] if whole else done.at[s, :, part]
            pltpu.make_async_copy(every, every, back_recv.at[s, part]).wait()


def per_device(
    latent, w_small, w_large, gain_embed, gain_attn, w_qkv, pos_bias, w_proj, gain_mlp, w_up, w_down
):
    row_count = lax.axis_size("rows")
    col_count = lax.axis_size("cols")
    samples, rows, cols, chan = latent.shape
    tile_rows, tile_cols = rows // 2, cols // 2
    feat = gain_embed.shape[0]
    half = feat // 2
    members = pos_bias.shape[1]
    phases = row_count // (members // col_count)
    share = tile_rows * tile_cols // STAGES // members
    groups = max(8, min(share, 256 // members))
    pixels = pltpu.VMEM((2, tile_rows + 1, tile_cols, 2 * chan), BF16)
    lines = max(1, share // (tile_cols // 2))
    exchange = pltpu.VMEM((STAGES, members, lines, share // groups // lines, groups, feat), F32)
    dma = pltpu.SemaphoreType.DMA
    inputs = (
        latent[0], w_small, w_large, gain_embed[None], gain_attn[None], w_qkv, pos_bias, w_proj,
        gain_mlp[None], w_up, w_down,
    )
    halves = lambda *shape: pltpu.VMEM((2,) + shape, BF16)
    out_bytes = tile_rows * tile_cols * feat * 4
    out = pl.pallas_call(
        functools.partial(block_kernel, (row_count, col_count, members, phases, groups)),
        name="crossformer_block",
        out_shape=pltpu.VMEM((tile_rows // lines, lines, tile_cols // groups, groups, feat), F32),
        in_specs=[pl.BlockSpec(memory_space=pltpu.HBM)] * 11,
        out_specs=pl.BlockSpec(memory_space=pltpu.VMEM),
        scratch_shapes=[pltpu.VMEM((rows + 2, cols + 16, chan), F32)]
        + [pltpu.VMEM(array.shape, F32) for array in inputs[1:]]
        + [
            pixels, pixels, pixels, pixels,
            halves(2, 2 * chan, feat),
            halves(2, 2 * chan, half),
            halves(4, 2 * chan, half),
            halves(*w_qkv.shape),
            halves(*w_proj.shape),
            halves(*w_up.shape),
            halves(*w_down.shape),
            pltpu.VMEM((HEADS, members * LANES, members * LANES), F32),
            exchange, exchange, exchange,
            pltpu.VMEM((2, rows, chan), F32),
            pltpu.VMEM((2, rows, chan), F32),
            dma((8,)), dma((8,)),
            dma((STAGES,)), dma((STAGES,)),
            dma((STAGES, lines)), dma((STAGES, lines)),
            dma((11,)), dma((8,)),
            pltpu.SemaphoreType.REGULAR,
        ],
        compiler_params=pltpu.CompilerParams(
            collective_id=0, has_side_effects=True, vmem_limit_bytes=67043328 - out_bytes
        ),
    )(*inputs)
    return out.reshape(samples, tile_rows, tile_cols, feat)


def solution(mesh):
    in_specs = (P(None, "rows", "cols", None),) + (P(),) * 10
    out_specs = P(None, "rows", "cols", None)
    return jax.shard_map(
        per_device, mesh=mesh, in_specs=in_specs, out_specs=out_specs, check_vma=False
    )
```
